32 devices in a mesh: particle: 4 (over x, core), rows: 8 (over z, y).
Axes of the slice: x: 2, y: 2, z: 4, core: 2. Of those that a mesh axis runs over, the one named last changes fastest.
Arguments:
- latent: bfloat16 [4, 32, 24, 640], P('particle', 'rows'), may hold values from -20 to 20
- ada_scale: float32 [640], replicated, may hold values from -0.5 to 0.5
- ada_shift: float32 [640], replicated, may hold values from -3 to 3
- conv_weight: bfloat16 [5760, 640], P('rows'), may hold values from -0.078125 to 0.078125
- qkv_weight: bfloat16 [640, 1920], replicated, may hold values from -1.4230249 to 1.4230249
- out_weight: bfloat16 [640, 640], replicated, may hold values from -0.25 to 0.25
- ancestors: int32 [4], replicated, may hold values from 0 to 3
Outputs:
- resampled: bfloat16 [4, 32, 24, 640], P('particle', 'rows')
The draws below stay inside these ranges and needn't reach their ends.
All inputs are finite; a program needn't handle non-finite values.
Results may differ from the reference program's by a relative error of at most 0.0081.
Values may be sent and summed in bfloat16 or wider, within the bound.
A program may use at most 64 MiB of HBM per device.

```python
import math
import jax
import jax.numpy as jnp
from jax import lax

C = 640
HEADS = 10
GROUPS = 32
W = 24
H = 32
PARTICLES = 4


def draw_latent(key, part):
    key_z, key_c = jax.random.split(key, 2)
    row_scale = 0.5 * 3.0 ** (jnp.arange(H, dtype=jnp.float32) / max(H - 1, 1))
    chan_scale = jnp.exp(jax.random.uniform(key_c, (C,), jnp.float32, math.log(0.3), math.log(3.0)))
    base = jnp.clip(jax.random.normal(key_z, (PARTICLES, H, W, C), jnp.float32), -4.0, 4.0)
    return (base * row_scale[None, :, None, None] * chan_scale).astype(jnp.bfloat16)


def draw_qkv_weight(key, part):
    base = jnp.clip(jax.random.normal(key, (C, 3 * C), jnp.float32), -6.0, 6.0) / math.sqrt(C)
    return base.astype(jnp.bfloat16)


def place_ends(result, own_key, smallest, largest):
    longest = result.shape.index(max(result.shape))
    spots = []
    for shift in (0, 1):
        where = [jax.random.randint(jax.random.fold_in(own_key, axis), (), 0, length) for axis, length in enumerate(result.shape)]
        where[longest] = (where[longest] + shift) % result.shape[longest]
        spots.append(tuple(where))
    return result.at[spots[0]].set(smallest).at[spots[1]].set(largest)


def steps_of(key, extent, cuts, low, largest):
    level, own = 1.0, jax.random.fold_in(key, 6)
    for dim, blocks in cuts:
        steps = jnp.exp(jax.random.uniform(jax.random.fold_in(own, dim), (blocks,), jnp.float32, low / len(cuts), largest / len(cuts)))
        level = level * jnp.repeat(steps, extent[dim] // blocks).reshape([-1 if axis == dim else 1 for axis in range(len(extent))])
    return level


def noise(rng, shape, deviation, limit, pieces=(), held_as=jnp.bfloat16):
    entries = jax.random.normal(rng, shape, jnp.float32) * deviation
    if len(pieces) > 0:
        entries = steps_of(rng, shape, pieces, -0.22, 0.18) * entries
    return jnp.clip(entries, min=-limit, max=limit).astype(held_as)


def setup_inputs(seed: int = 0) -> dict:
    streams_of = jax.random.split(jax.random.key(seed), 8)
    latent = draw_latent(jax.random.fold_in(streams_of[7], 71), 0)
    ada_scale = jnp.clip(jax.random.uniform(streams_of[1], (C,), jnp.float32, -0.5, 0.5), -0.5, 0.5)
    ada_shift = noise(streams_of[2], (C,), 0.5, 3.0, (), jnp.float32)
    conv_weight = noise(streams_of[3], (9 * C, C), (9 * C) ** -0.5, 0.078125, ((0, 8),))
    qkv_weight = draw_qkv_weight(jax.random.fold_in(streams_of[7], 71), 0)
    out_weight = noise(streams_of[5], (C, C), C ** -0.5, 0.25)
    ancestors = place_ends(jax.random.randint(streams_of[6], (PARTICLES,), 0, PARTICLES), jax.random.fold_in(streams_of[6], 1), 0, PARTICLES - 1).astype(jnp.int32)
    return {"latent": latent, "ada_scale": ada_scale, "ada_shift": ada_shift, "conv_weight": conv_weight, "qkv_weight": qkv_weight, "out_weight": out_weight, "ancestors": ancestors}


def group_norm(values):
    grouped = values.reshape(values.shape[0], GROUPS, -1)
    count = grouped.shape[0] * grouped.shape[2]
    mean_g = lax.optimization_barrier(jnp.sum(grouped, axis=(0, 2))) / count
    square_g = lax.optimization_barrier(jnp.sum(grouped * grouped, axis=(0, 2))) / count
    inverse = lax.rsqrt(square_g - mean_g * mean_g + 1e-05)
    per_group = C // GROUPS
    return (values - jnp.repeat(mean_g, per_group)) * jnp.repeat(inverse, per_group)

def reference(latent, ada_scale, ada_shift, conv_weight, qkv_weight, out_weight, ancestors):
    head_dim = C // HEADS

    def heads_of(block):
        return block.reshape(H * W, HEADS, head_dim).transpose(1, 0, 2)

    def one_head(triple):
        query_h, key_h, value_h = triple
        scores = jnp.dot(query_h, key_h.T, preferred_element_type=jnp.float32) * head_dim ** (-0.5)
        top = lax.optimization_barrier(jnp.max(scores, axis=1, keepdims=True))
        weights = jnp.exp(scores - top)
        total = lax.optimization_barrier(jnp.sum(weights, axis=1, keepdims=True))
        return jnp.dot(weights.astype(jnp.bfloat16), value_h, preferred_element_type=jnp.float32) / total

    def one_particle(latent_p):
        field = latent_p.astype(jnp.float32).reshape(H * W, C)
        active = jax.nn.silu(group_norm(field) * (1.0 + ada_scale) + ada_shift).astype(jnp.bfloat16)
        padded = jnp.pad(active.reshape(H, W, C), ((1, 1), (1, 1), (0, 0)))
        conv = jnp.zeros((H * W, C), jnp.float32)
        for row_off in range(3):
            for col_off in range(3):
                tap = row_off * 3 + col_off
                window = padded[row_off:row_off + H, col_off:col_off + W].reshape(H * W, C)
                conv = conv + jnp.dot(window, conv_weight[tap * C:(tap + 1) * C], preferred_element_type=jnp.float32)
        resid = lax.optimization_barrier((field + conv).astype(jnp.bfloat16))
        normed = group_norm(resid.astype(jnp.float32)).astype(jnp.bfloat16)
        project = jnp.dot(normed, qkv_weight, preferred_element_type=jnp.float32).astype(jnp.bfloat16)
        triple = (heads_of(project[:, :C]), heads_of(project[:, C:2 * C]), heads_of(project[:, 2 * C:]))
        mixed = lax.map(one_head, triple)
        attended = mixed.transpose(1, 0, 2).reshape(H * W, C).astype(jnp.bfloat16)
        output = resid.astype(jnp.float32) + jnp.dot(attended, out_weight, preferred_element_type=jnp.float32)
        return output.astype(jnp.bfloat16).reshape(H, W, C)
    blocks = lax.map(one_particle, latent)
    return jnp.take(blocks, ancestors.astype(jnp.int32), axis=0)
```

```python
import functools
import math

import jax
import jax.numpy as jnp
from jax import lax
from jax.experimental import pallas as pl
from jax.experimental.pallas import tpu as pltpu
from jax.sharding import PartitionSpec as P

HEADS = 10
GROUPS = 32
INNER = 2
CORES = 2
LANES = 128
GRAIN = 16
TAPS = 9
MESH = pl.DeviceIdType.MESH
NT = (((1,), (1,)), ((), ()))
HIGH = lax.Precision.HIGHEST


def cut_rows(rows, pieces):
    grains = rows // GRAIN
    pieces = min(pieces, grains)
    tail = max(1, grains // 6) if pieces > 1 else grains
    rest = grains - tail
    cuts, at = [], 0
    for i in range(pieces - 1):
        take = -(-rest // (pieces - 1 - i))
        cuts.append((at * GRAIN, take * GRAIN))
        at += take
        rest -= take
    cuts.append((at * GRAIN, tail * GRAIN))
    return cuts


def kernel(
    dims,
    anc_ref,
    x_ref,
    scale_ref,
    shift_ref,
    wconv_hbm,
    wqkv_hbm,
    wout_hbm,
    out_ref,
    wz,
    wt,
    wbuf,
    wd,
    wqkv,
    wpad,
    wkvt,
    wout,
    lat,
    act,
    yt,
    field,
    chunk,
    rt,
    nt,
    kvt,
    att,
    blk,
    blocks,
    stat_own,
    stats,
    load_sem,
    ws,
    wr,
    ss,
    sr,
    up1,
    down1,
    ys1,
    rv1,
    up2,
    down2,
    ys2,
    rv2,
    ps,
    pr,
):
    rows_here, width, chans, ranks, particles, share, aligned = dims
    tokens = rows_here * width
    total = tokens * ranks
    outer = ranks // INNER
    groups = particles // CORES
    cs = chans // ranks
    csp = chunk.shape[0]
    cpad = ranks * csp
    per_group = chans // GROUPS
    count = total * per_group
    head_dim = chans // HEADS
    tiles = chans // LANES
    bf16, f32 = jnp.bfloat16, jnp.float32
    me = lax.axis_index("rows")
    mine = lax.axis_index("particle")
    a = lax.div(me, INNER)
    b = lax.rem(me, INNER)
    other = a * INNER + (1 - b)
    grp = lax.div(mine, CORES)
    core = lax.rem(mine, CORES)

    if aligned:
        skip = lax.rem(me * share, LANES)
        conv_in = wz.at[pl.ds(pl.multiple_of(skip, GRAIN), share)]
    else:
        conv_in = wz
    qkv_in = wqkv if cpad == chans else wpad
    loads = [
        pltpu.make_async_copy(wconv_hbm, conv_in, load_sem.at[0]),
        pltpu.make_async_copy(wqkv_hbm, qkv_in, load_sem.at[1]),
        pltpu.make_async_copy(wout_hbm, wout, load_sem.at[2]),
    ]
    for load in loads:
        load.start()

    barrier = pltpu.get_barrier_semaphore()
    for k in range(1, ranks):
        pl.semaphore_signal(
            barrier, inc=1, device_id={"rows": lax.rem(me + k, ranks)}, device_id_type=MESH
        )
    for k in range(1, particles):
        pl.semaphore_signal(
            barrier,
            inc=1,
            device_id={"particle": lax.rem(mine + k, particles)},
            device_id_type=MESH,
        )

    if aligned:
        lowest = min(share * r % LANES for r in range(ranks))
        highest = max(share * r % LANES for r in range(ranks))
        for i in range(wz.shape[0] // GRAIN):
            if i * GRAIN >= highest and (i + 1) * GRAIN <= lowest + share:
                continue

            @pl.when((skip > i * GRAIN) | (skip + share <= i * GRAIN))
            def _():
                wz[i * GRAIN : (i + 1) * GRAIN] = jnp.zeros((GRAIN, chans), bf16)

    chan_r = lax.broadcasted_iota(jnp.int32, (chans, LANES), 0)
    group_r = lax.broadcasted_iota(jnp.int32, (chans, LANES), 1) * per_group
    inside = (chan_r >= group_r) & (chan_r < group_r + per_group)
    to_group = jnp.where(inside, 1.0, 0.0).astype(f32)
    group_c = lax.broadcasted_iota(jnp.int32, (LANES, chans), 0) * per_group
    chan_c = lax.broadcasted_iota(jnp.int32, (LANES, chans), 1)
    inside = (chan_c >= group_c) & (chan_c < group_c + per_group)
    to_chan = jnp.where(inside, 1.0, 0.0).astype(f32)

    x32 = x_ref[...].astype(f32)
    sums = jnp.concatenate(
        [
            jnp.sum(x32, axis=0, keepdims=True),
            jnp.sum(x32 * x32, axis=0, keepdims=True),
            jnp.zeros((6, chans), f32),
        ],
        axis=0,
    )
    stat_own[...] = jnp.dot(sums, to_group, precision=HIGH, preferred_element_type=f32)
    stats[me] = stat_own[...]

    with jax.named_scope("barrier"):
        pl.semaphore_wait(barrier, ranks + particles - 2)

    def remote(src, dst, send, recv, where):
        return pltpu.make_async_remote_copy(
            src_ref=src,
            dst_ref=dst,
            send_sem=send,
            recv_sem=recv,
            device_id=where,
            device_id_type=MESH,
        )

    class Gather:
        def __init__(self, src, buf, rows, cuts, up, down, across, rv):
            self.src, self.buf, self.rows, self.cuts = src, buf, rows, cuts
            self.up, self.down, self.across, self.rv = up, down, across, rv
            self.last = len(cuts) - 1

        def part(self, slot, i):
            start, size = self.cuts[i]
            return self.buf.at[pl.ds(pl.multiple_of(slot * self.rows + start, GRAIN), size)]

        def copy(self, slot, i, sems, row, own=False):
            start, size = self.cuts[i]
            here = self.src.at[pl.ds(start, size)] if own else self.part(slot, i)
            return remote(
                here, self.part(slot, i), sems.at[slot, i], self.rv.at[slot, i], {"rows": row}
            )

        def both(self, slot, i, do, own=False):
            @pl.when(a + 1 < outer)
            def _():
                do(self.copy(slot, i, self.up, (a + 1) * INNER + b, own))

            @pl.when(a > 0)
            def _():
                do(self.copy(slot, i, self.down, (a - 1) * INNER + b, own))

        def arrived(self, slot, i):
            self.copy(slot, i, self.across, other).wait_recv()

        def sides(self, t):
            return (
                (a >= t, a - t, a + 1 < outer, self.up, a + 1),
                (a + t < outer, a + t, a > 0, self.down, a - 1),
            )

        def begin(self):
            for i in [self.last] + list(range(self.last)):
                self.copy(me, i, self.across, other, True).start()
                self.both(me, i, lambda c: c.start(), True)
            self.buf[pl.ds(pl.multiple_of(me * self.rows, GRAIN), self.rows)] = self.src[...]

        def turn(self):
            self.arrived(other, self.last)
            self.both(other, self.last, lambda c: c.start())

        def step(self, t):
            for i in range(self.last + 1):
                for present, origin, onward, sems, target in self.sides(t):
                    near = origin * INNER + b

                    @pl.when(present)
                    def _():
                        self.arrived(near, i)

                    @pl.when(present & onward)
                    def _():
                        self.copy(near, i, sems, target * INNER + b).start()

                    if i < self.last:

                        @pl.when(present)
                        def _():
                            self.copy(near, i, self.across, other).start()

            for present, origin, onward, sems, target in self.sides(t):
                far = origin * INNER + (1 - b)

                @pl.when(present)
                def _():
                    self.arrived(far, self.last)

                @pl.when(present & onward)
                def _():
                    self.copy(far, self.last, sems, target * INNER + b).start()

        def rest(self, t):
            for present, origin, _, _, _ in self.sides(t) if t else ((None, a, 0, 0, 0),):
                far = origin * INNER + (1 - b)
                for i in range(self.last):
                    if present is None:
                        self.arrived(far, i)
                    else:

                        @pl.when(present)
                        def _():
                            self.arrived(far, i)

        def finish(self):
            def done(c):
                c.wait_send()

            for i in range(self.last + 1):
                self.copy(me, i, self.across, other, True).wait_send()
                self.both(me, i, done, True)
            self.both(other, self.last, done)
            for t in range(1, outer):
                for present, origin, onward, sems, target in self.sides(t):
                    near = origin * INNER + b
                    far = origin * INNER + (1 - b)

                    @pl.when(present & onward)
                    def _():
                        for i in range(self.last + 1):
                            self.copy(near, i, sems, target * INNER + b).wait_send()
                        self.copy(far, self.last, sems, target * INNER + b).wait_send()

                    @pl.when(present)
                    def _():
                        for i in range(self.last):
                            self.copy(near, i, self.across, other).wait_send()

    def each_slot(t, fn):
        if t == 0:
            fn(me)
            fn(other)
            return
        for present, origin in ((a >= t, a - t), (a + t < outer, a + t)):

            @pl.when(present)
            def _():
                fn(origin * INNER + b)
                fn(origin * INNER + (1 - b))

    first = Gather(x_ref, lat, tokens, cut_rows(tokens, dims_pieces(outer)), up1, down1, ys1, rv1)
    second = Gather(chunk, rt, csp, cut_rows(csp, dims_pieces(outer)), up2, down2, ys2, rv2)

    def stat_copy(k):
        return remote(
            stat_own, stats.at[me], ss.at[k - 1], sr.at[me], {"rows": lax.rem(me + k, ranks)}
        )

    def stat_from(k):
        row = lax.rem(me + ranks - k, ranks)
        return remote(stat_own, stats.at[row], ss.at[k - 1], sr.at[row], {"rows": row})

    def w_copy(k):
        dest = lax.rem(me + k, ranks)
        return remote(wt.at[dest], wbuf.at[me], ws.at[k - 1, 0], wr.at[me], {"rows": dest})

    def w_slot(k):
        return lax.rem(me + ranks - k, ranks)

    def w_pass_on(k, j, where):
        slot = w_slot(k)
        return remote(wbuf.at[slot], wbuf.at[slot], ws.at[k - 1, j], wr.at[slot], where)

    def w_arrived(k):
        w_pass_on(k, 1, {"rows": other}).wait_recv()

    def w_to_core(k):
        return w_pass_on(k, 1, {"particle": grp * CORES + (1 - core)})

    def w_to_group(k, g):
        return w_pass_on(k, 1 + g, {"particle": lax.rem(grp + g, groups) * CORES + core})

    with jax.named_scope("start"):
        first.begin()
        for k in range(1, ranks):
            stat_copy(k).start()
        loads[0].wait()
        turned = wz[...].T
        for d in range(ranks):
            wt[d, 0:cs] = turned[d * cs : (d + 1) * cs]
            if csp != cs:
                wt[d, cs:csp] = jnp.zeros((csp - cs, wt.shape[2]), bf16)
        for k in range(1, ranks):

            @pl.when(mine == k % particles)
            def _():
                w_copy(k).start()

        wbuf[me] = wt[me]
        first.turn()

    def w_forward(k):
        q = k % particles

        @pl.when(mine == q)
        def _():
            w_arrived(k)
            for g in range(1, groups):
                w_to_group(k, g).start()
            w_to_core(k).start()

    def w_relay(k):
        q = k % particles

        @pl.when((core == q % CORES) & (grp != q // CORES))
        def _():
            w_arrived(k)
            w_to_core(k).start()

    def w_last(k):
        q = k % particles

        @pl.when(core != q % CORES)
        def _():
            w_arrived(k)

    with jax.named_scope("stats"):
        for k in range(1, ranks):
            stat_from(k).wait_recv()
        by_group = jnp.sum(stats[...], axis=0) / count
        mean_g = by_group[0:1]
        inverse = lax.rsqrt(by_group[1:2] - mean_g * mean_g + 1e-05)
        back = jnp.concatenate([mean_g, inverse, jnp.zeros((6, LANES), f32)], axis=0)
        spread = jnp.dot(back, to_chan, precision=HIGH, preferred_element_type=f32)
        mean_c, inverse_c = spread[0:1], spread[1:2]
        gain = 1.0 + scale_ref[...].reshape(1, chans)
        bias = shift_ref[...].reshape(1, chans)

    def activate(slot):
        at = pl.ds(pl.multiple_of(slot * tokens, GRAIN), tokens)
        v = lat[at].astype(f32)
        v = (v - mean_c) * inverse_c * gain + bias
        act[at] = (v / (1.0 + jnp.exp(-v))).astype(bf16)

    half = total // 2
    near_half = outer // 2
    mine_half = lax.div(a, near_half)

    def conv(which):
        at = pl.multiple_of(which * half, LANES)
        yt[:, pl.ds(at, half)] = lax.dot_general(
            wd[...], act[pl.ds(at, half)], NT, preferred_element_type=f32
        )

    with jax.named_scope("g1a"):
        for t in range(1, near_half):
            first.step(t)
    with jax.named_scope("w1"):
        for k in range(1, ranks):
            w_forward(k)
    with jax.named_scope("g1b"):
        for t in range(near_half, outer):
            first.step(t)
    with jax.named_scope("w2"):
        for k in range(1, ranks):
            w_relay(k)
    with jax.named_scope("act1"):
        activate(me)
        first.rest(0)
        activate(other)
        for t in range(1, outer):
            first.rest(t)
            each_slot(t, activate)
    with jax.named_scope("w3"):
        for k in range(1, ranks):
            w_last(k)
    with jax.named_scope("wd"):
        for tap in range(TAPS):
            for j in range(tiles):
                tile = tap * tiles + j
                part = None
                for r in range(ranks):
                    if share * r < LANES * (tile + 1) and share * (r + 1) > LANES * tile:
                        i = tile - share * r // LANES
                        piece = wbuf[r, :, i * LANES : (i + 1) * LANES]
                        part = piece if part is None else part + piece
                wd[tap * csp : (tap + 1) * csp, j * LANES : (j + 1) * LANES] = part
    with jax.named_scope("conv"):
        pick = lax.broadcasted_iota(jnp.int32, (csp, chans), 0)
        at = lax.broadcasted_iota(jnp.int32, (csp, chans), 1)
        pick = jnp.where((at == me * cs + pick) & (pick < cs), 1.0, 0.0).astype(bf16)
        field[...] = lax.dot_general(pick, lat[...], NT, preferred_element_type=f32)
        conv(mine_half)
        conv(1 - mine_half)

    with jax.named_scope("taps"):
        lane = lax.broadcasted_iota(jnp.int32, (1, total), 1)
        column = lax.rem(lane, width)
        has_left = column > 0
        has_right = column < width - 1
        has_above = lane >= width
        has_below = lane < total - width

        def add_taps(i, carry):
            def tap(row, col):
                base = (row * 3 + col) * csp
                return yt[pl.ds(pl.multiple_of(base + i * GRAIN, GRAIN), GRAIN), :]

            cols = []
            for col in range(3):
                above = jnp.where(has_above, pltpu.roll(tap(0, col), width, 1), 0.0)
                below = jnp.where(has_below, pltpu.roll(tap(2, col), total - width, 1), 0.0)
                cols.append(tap(1, col) + above + below)
            left = jnp.where(has_left, pltpu.roll(cols[0], 1, 1), 0.0)
            right = jnp.where(has_right, pltpu.roll(cols[2], total - 1, 1), 0.0)
            at = pl.ds(pl.multiple_of(i * GRAIN, GRAIN), GRAIN)
            chunk[at] = (field[at] + (cols[1] + left + right)).astype(bf16)
            return carry

        lax.fori_loop(0, csp // GRAIN, add_taps, 0)

    own_r = lax.broadcasted_iota(jnp.int32, (csp, csp), 0)
    own_c = lax.broadcasted_iota(jnp.int32, (csp, csp), 1)
    same = (lax.div(own_r, per_group) == lax.div(own_c, per_group)) & (own_r < cs) & (own_c < cs)
    same = jnp.where(same, 1.0, 0.0).astype(f32)
    lane = lax.broadcasted_iota(jnp.int32, (csp, LANES), 1)

    def normalize(slot):
        at = pl.ds(pl.multiple_of(slot * csp, GRAIN), csp)
        v = rt[at].astype(f32)
        both = jnp.where(
            lane == 0,
            jnp.sum(v, axis=1, keepdims=True),
            jnp.where(lane == 1, jnp.sum(v * v, axis=1, keepdims=True), 0.0),
        )
        both = jnp.dot(same, both, precision=HIGH, preferred_element_type=f32) / count
        mean = both[:, 0:1]
        inv = lax.rsqrt(both[:, 1:2] - mean * mean + 1e-05)
        nt[at] = ((v - mean) * inv).astype(bf16)

    with jax.named_scope("g2"):
        second.begin()
        loads[1].wait()
        if cpad != chans:
            wqkv[...] = jnp.zeros_like(wqkv)
            for d in range(ranks):
                wqkv[d * csp : d * csp + cs] = wpad[d * cs : (d + 1) * cs]
        for n in range(2 * tiles):
            wkvt[n * LANES : (n + 1) * LANES] = wqkv[
                :, chans + n * LANES : chans + (n + 1) * LANES
            ].T
        second.turn()
        normalize(me)
        for t in range(1, outer):
            second.step(t)
        second.rest(0)
        normalize(other)
        for t in range(1, outer):
            second.rest(t)
            each_slot(t, normalize)

    with jax.named_scope("qkv"):
        step = 2 * LANES
        for n in range(2 * chans // step):
            kvt[n * step : (n + 1) * step] = jnp.dot(
                wkvt[n * step : (n + 1) * step], nt[...], preferred_element_type=f32
            ).astype(bf16)
        row = lax.broadcasted_iota(jnp.int32, (tokens, total), 0)
        at = lax.broadcasted_iota(jnp.int32, (tokens, total), 1)
        pick = jnp.where(at == me * tokens + row, 1.0, 0.0).astype(bf16)
        mine_n = lax.dot_general(pick, nt[...], NT, preferred_element_type=f32).astype(bf16)
        resid = lax.dot_general(pick, rt[...], NT, preferred_element_type=f32)
        if cpad != chans:
            resid = jnp.concatenate(
                [resid[:, d * csp : d * csp + cs] for d in range(ranks)], axis=1
            )
        query = jnp.dot(mine_n, wqkv[:, :chans], preferred_element_type=f32).astype(bf16)

    with jax.named_scope("attn"):
        pair = 2 * head_dim
        lane = lax.broadcasted_iota(jnp.int32, (tokens, pair), 1)
        low = lane < head_dim
        zero = jnp.zeros((tokens, pair), bf16)
        for h in range(HEADS // 2):
            q = query[:, h * pair : (h + 1) * pair]
            q = jnp.concatenate([jnp.where(low, q, zero), jnp.where(low, zero, q)], axis=0)
            scores = jnp.dot(
                q, kvt[h * pair : (h + 1) * pair], preferred_element_type=f32
            ) * (head_dim ** (-0.5))
            top = jnp.max(scores, axis=1, keepdims=True)
            weights = jnp.exp(scores - top)
            norm = jnp.sum(weights, axis=1, keepdims=True)
            mixed = (
                lax.dot_general(
                    weights.astype(bf16),
                    kvt[chans + h * pair : chans + (h + 1) * pair],
                    NT,
                    preferred_element_type=f32,
                )
                / norm
            )
            att[:, h * pair : (h + 1) * pair] = jnp.where(
                low, mixed[:tokens], mixed[tokens:]
            ).astype(bf16)
    with jax.named_scope("proj"):
        loads[2].wait()
        block = (resid + jnp.dot(att[...], wout[...], preferred_element_type=f32)).astype(bf16)
        blk[...] = block
        blocks[mine] = block

    def to_particle(k):
        peer = lax.rem(mine + k, particles)
        return remote(blk, blocks.at[mine], ps.at[k - 1], pr.at[k - 1], {"particle": peer})

    with jax.named_scope("resample"):
        for k in range(1, particles):
            to_particle(k).start()
        for k in range(1, particles):
            to_particle(k).wait_recv()
        out_ref[...] = blocks[anc_ref[mine]]
    with jax.named_scope("drain"):
        for k in range(1, particles):
            to_particle(k).wait_send()
        first.finish()
        second.finish()
        for k in range(1, ranks):
            stat_copy(k).wait_send()
            q = k % particles

            @pl.when(mine == q)
            def _():
                w_copy(k).wait_send()
                for g in range(1, groups):
                    w_to_group(k, g).wait_send()

            @pl.when(core == q % CORES)
            def _():
                w_to_core(k).wait_send()


def dims_pieces(outer):
    return 3 if outer <= 4 else 2


def per_device(latent, ada_scale, ada_shift, conv_weight, qkv_weight, out_weight, ancestors):
    _, rows_here, width, chans = latent.shape
    tokens = rows_here * width
    ranks = lax.axis_size("rows")
    particles = lax.axis_size("particle")
    groups = particles // CORES
    total = tokens * ranks
    share = conv_weight.shape[0]
    span = max(-(-(share * r % LANES + share) // LANES) for r in range(ranks)) * LANES
    aligned = math.gcd(share, LANES) % GRAIN == 0
    if not aligned:
        start = lax.rem(lax.axis_index("rows") * share, LANES)
        conv_weight = lax.dynamic_update_slice(
            jnp.zeros((span, chans), conv_weight.dtype), conv_weight, (start, 0)
        )
    cs = chans // ranks
    csp = -(-cs // GRAIN) * GRAIN
    cpad = csp * ranks
    pieces = dims_pieces(ranks // INNER)
    n1 = len(cut_rows(tokens, pieces))
    n2 = len(cut_rows(csp, pieces))
    dims = (rows_here, width, chans, ranks, particles, share, aligned)
    bf16, f32 = jnp.bfloat16, jnp.float32
    dma = pltpu.SemaphoreType.DMA
    out = pl.pallas_call(
        functools.partial(kernel, dims),
        out_shape=jax.ShapeDtypeStruct((tokens, chans), bf16),
        in_specs=[pl.BlockSpec(memory_space=pltpu.SMEM)]
        + [pl.BlockSpec(memory_space=pltpu.VMEM)] * 3
        + [pl.BlockSpec(memory_space=pl.ANY)] * 3,
        out_specs=pl.BlockSpec(memory_space=pltpu.VMEM),
        scratch_shapes=[
            pltpu.VMEM((span, chans), bf16),
            pltpu.VMEM((ranks, csp, span), bf16),
            pltpu.VMEM((ranks, csp, span), bf16),
            pltpu.VMEM((TAPS * csp, chans), bf16),
            pltpu.VMEM((cpad, 3 * chans), bf16),
            pltpu.VMEM((GRAIN, LANES) if cpad == chans else qkv_weight.shape, bf16),
            pltpu.VMEM((2 * chans, cpad), bf16),
            pltpu.VMEM(out_weight.shape, bf16),
            pltpu.VMEM((total, chans), bf16),
            pltpu.VMEM((total, chans), bf16),
            pltpu.VMEM((TAPS * csp, total), f32),
            pltpu.VMEM((csp, total), f32),
            pltpu.VMEM((csp, total), bf16),
            pltpu.VMEM((cpad, total), bf16),
            pltpu.VMEM((cpad, total), bf16),
            pltpu.VMEM((2 * chans, total), bf16),
            pltpu.VMEM((tokens, chans), bf16),
            pltpu.VMEM((tokens, chans), bf16),
            pltpu.VMEM((particles, tokens, chans), bf16),
            pltpu.VMEM((8, LANES), f32),
            pltpu.VMEM((ranks, 8, LANES), f32),
            dma((3,)),
            dma((ranks, 1 + groups)),
            dma((ranks,)),
            dma((ranks,)),
            dma((ranks,)),
            dma((ranks, n1)),
            dma((ranks, n1)),
            dma((ranks, n1)),
            dma((ranks, n1)),
            dma((ranks, n2)),
            dma((ranks, n2)),
            dma((ranks, n2)),
            dma((ranks, n2)),
            dma((particles,)),
            dma((particles,)),
        ],
        compiler_params=pltpu.CompilerParams(
            collective_id=0, has_side_effects=True, vmem_limit_bytes=64000 * 1024
        ),
        name="block",
    )(
        ancestors,
        latent.reshape(tokens, chans),
        ada_scale,
        ada_shift,
        conv_weight,
        qkv_weight,
        out_weight,
    )
    return out.reshape(latent.shape)


def solution(mesh):
    in_specs = (P("particle", "rows", None, None), P(), P(), P("rows", None), P(), P(), P())
    out_specs = P("particle", "rows", None, None)
    return jax.shard_map(
        per_device, mesh=mesh, in_specs=in_specs, out_specs=out_specs, check_vma=False
    )
```

```python
import functools
import math

import jax
import jax.numpy as jnp
from jax import lax
from jax.experimental import pallas as pl
from jax.experimental.pallas import tpu as pltpu
from jax.sharding import PartitionSpec as P

HEADS = 10
GROUPS = 32
INNER = 2
CUT1 = 2
CUT2 = 1
CORES = 2
LANES = 128
GRAIN = 16
TAPS = 9
MESH = pl.DeviceIdType.MESH
NT = (((1,), (1,)), ((), ()))
HIGH = lax.Precision.HIGHEST


def cut_rows(rows, grains):
    step = grains * GRAIN
    return [(at, min(step, rows - at)) for at in range(0, rows, step)]


def kernel(
    dims,
    anc_ref,
    x_hbm,
    scale_hbm,
    shift_hbm,
    wconv_hbm,
    wqkv_hbm,
    wout_hbm,
    out_ref,
    x_ref,
    scale_ref,
    shift_ref,
    wz,
    wt,
    wbuf,
    wd,
    wqkv,
    wpad,
    wkvt,
    wout,
    lat,
    act,
    yt,
    field,
    chunk,
    rt,
    nt,
    kvt,
    att,
    blocks,
    stat_own,
    stats,
    load_sem,
    ws,
    wr,
    ss,
    sent1,
    near1,
    far1,
    sent2,
    near2,
    far2,
    ps,
    pr,
):
    rows_here, width, chans, ranks, particles, share = dims
    tokens = rows_here * width
    total = tokens * ranks
    outer = ranks // INNER
    groups = particles // CORES
    cs = chans // ranks
    csp = chunk.shape[0]
    cpad = ranks * csp
    per_group = chans // GROUPS
    count = total * per_group
    head_dim = chans // HEADS
    tiles = chans // LANES
    bf16, f32 = jnp.bfloat16, jnp.float32
    me = lax.axis_index("rows")
    mine = lax.axis_index("particle")
    a = lax.div(me, INNER)
    b = lax.rem(me, INNER)
    other = a * INNER + (1 - b)
    grp = lax.div(mine, CORES)
    core = lax.rem(mine, CORES)

    conv_in = wz.at[0 : wconv_hbm.shape[0]]
    qkv_in = wqkv if cpad == chans else wpad
    loads = [
        pltpu.make_async_copy(wconv_hbm, conv_in, load_sem.at[0]),
        pltpu.make_async_copy(wqkv_hbm, qkv_in, load_sem.at[1]),
        pltpu.make_async_copy(wout_hbm, wout, load_sem.at[2]),
        pltpu.make_async_copy(x_hbm, x_ref, load_sem.at[3]),
        pltpu.make_async_copy(scale_hbm, scale_ref, load_sem.at[4]),
        pltpu.make_async_copy(shift_hbm, shift_ref, load_sem.at[5]),
    ]
    for i in (3, 0, 4, 5, 1, 2):
        loads[i].start()

    barrier = pltpu.get_barrier_semaphore()
    for k in range(1, ranks):
        pl.semaphore_signal(
            barrier, inc=1, device_id={"rows": lax.rem(me + k, ranks)}, device_id_type=MESH
        )
    for k in range(1, particles):
        pl.semaphore_signal(
            barrier,
            inc=1,
            device_id={"particle": lax.rem(mine + k, particles)},
            device_id_type=MESH,
        )

    if wz.shape[0] > wconv_hbm.shape[0]:
        tail = wz.shape[0] - wconv_hbm.shape[0]
        wz[wconv_hbm.shape[0] :] = jnp.zeros((tail, chans), bf16)

    chan_r = lax.broadcasted_iota(jnp.int32, (chans, LANES), 0)
    group_r = lax.broadcasted_iota(jnp.int32, (chans, LANES), 1) * per_group
    inside = (chan_r >= group_r) & (chan_r < group_r + per_group)
    to_group = jnp.where(inside, 1.0, 0.0).astype(f32)
    group_c = lax.broadcasted_iota(jnp.int32, (LANES, chans), 0) * per_group
    chan_c = lax.broadcasted_iota(jnp.int32, (LANES, chans), 1)
    inside = (chan_c >= group_c) & (chan_c < group_c + per_group)
    to_chan = jnp.where(inside, 1.0, 0.0).astype(f32)

    loads[3].wait()
    x32 = x_ref[...].astype(f32)
    sums = jnp.concatenate(
        [
            jnp.sum(x32, axis=0, keepdims=True),
            jnp.sum(x32 * x32, axis=0, keepdims=True),
            jnp.zeros((6, chans), f32),
        ],
        axis=0,
    )
    stat_own[...] = jnp.dot(sums, to_group, precision=HIGH, preferred_element_type=f32)
    stats[me] = stat_own[...]

    with jax.named_scope("turn"):
        loads[0].wait()
        turned = wz[...].T
        for d in range(ranks):
            wt[d, 0:cs] = turned[d * cs : (d + 1) * cs]
            if csp != cs:
                wt[d, cs:csp] = jnp.zeros((csp - cs, wt.shape[2]), bf16)

    with jax.named_scope("barrier"):
        pl.semaphore_wait(barrier, ranks + particles - 2)

    def remote(src, dst, send, recv, where):
        return pltpu.make_async_remote_copy(
            src_ref=src,
            dst_ref=dst,
            send_sem=send,
            recv_sem=recv,
            device_id=where,
            device_id_type=MESH,
        )

    class Gather:
        def __init__(self, src, buf, rows, cuts, sent, near, far):
            self.src, self.buf, self.rows, self.cuts = src, buf, rows, cuts
            self.sent, self.near, self.far = sent, near, far
            self.pieces = range(len(cuts))

        def rows_of(self, slot, start, size):
            return self.buf.at[pl.ds(pl.multiple_of(slot * self.rows + start, GRAIN), size)]

        def onto(self, origin, i, side, own=False):
            start, size = self.cuts[i]
            dst = self.rows_of(origin * INNER + b, start, size)
            src = self.src.at[pl.ds(start, size)] if own else dst
            recv = self.near.at[origin, i] if side else self.far.at[origin]
            row = (a + side) * INNER + b if side else other
            return remote(src, dst, self.sent.at[side + 1], recv, {"rows": row})

        def pass_on(self, origin, i, side, own=False):
            onward = (a + 1 < outer) if side == 1 else (a > 0)

            @pl.when(onward)
            def _():
                self.onto(origin, i, side, own).start()

        def begin(self, pieces):
            for i in pieces:
                self.onto(a, i, 0, True).start()
                self.pass_on(a, i, 1, True)
                self.pass_on(a, i, -1, True)

        def keep(self):
            self.buf[pl.ds(pl.multiple_of(me * self.rows, GRAIN), self.rows)] = self.src[...]

        def step(self, t):
            for i in self.pieces:
                for present, origin, side in ((a >= t, a - t, 1), (a + t < outer, a + t, -1)):

                    @pl.when(present)
                    def _():
                        self.onto(origin, i, 1).wait_recv()
                        self.pass_on(origin, i, side)
                        self.onto(origin, i, 0).start()

        def far_slab(self, origin):
            slab = self.rows_of(origin * INNER + (1 - b), 0, self.rows)
            remote(slab, slab, self.sent.at[1], self.far.at[origin], {"rows": other}).wait_recv()

        def rest(self, t):
            if t == 0:
                self.far_slab(a)
                return
            for present, origin in ((a >= t, a - t), (a + t < outer, a + t)):

                @pl.when(present)
                def _():
                    self.far_slab(origin)

        def sent_all(self, side, slabs):
            part = self.buf.at[0 : slabs * self.rows]
            remote(part, part, self.sent.at[side + 1], self.far.at[0], {"rows": other}).wait_send()

        def finish(self):
            self.sent_all(0, outer)
            for v in range(outer):

                @pl.when(a == v)
                def _():
                    if v + 1 < outer:
                        self.sent_all(1, v + 1)
                    if v > 0:
                        self.sent_all(-1, outer - v)

    def each_slot(t, fn):
        if t == 0:
            fn(me)
            fn(other)
            return
        for present, origin in ((a >= t, a - t), (a + t < outer, a + t)):

            @pl.when(present)
            def _():
                fn(origin * INNER + b)
                fn(origin * INNER + (1 - b))

    near_half = outer // 2
    first = Gather(x_ref, lat, tokens, cut_rows(tokens, CUT1), sent1, near1, far1)
    second = Gather(chunk, rt, csp, cut_rows(csp, CUT2), sent2, near2, far2)

    def stat_copy(k):
        return remote(
            stat_own, stats.at[me], ss.at[0], ss.at[1], {"rows": lax.rem(me + k, ranks)}
        )

    def stat_all():
        part = stats.at[0 : ranks - 1]
        return remote(part, part, ss.at[0], ss.at[1], {"rows": other})

    def w_copy(k):
        dest = lax.rem(me + k, ranks)
        return remote(wt.at[dest], wbuf.at[me], ws.at[0], wr.at[me], {"rows": dest})

    def w_slot(k):
        return lax.rem(me + ranks - k, ranks)

    def w_pass_on(k, j, where):
        slot = w_slot(k)
        return remote(wbuf.at[slot], wbuf.at[slot], ws.at[j], wr.at[slot], where)

    def w_arrived(k):
        w_pass_on(k, 1, {"rows": other}).wait_recv()

    def w_to_core(k):
        return w_pass_on(k, 1, {"particle": grp * CORES + (1 - core)})

    def w_to_group(k, g):
        return w_pass_on(k, 1 + g, {"particle": lax.rem(grp + g, groups) * CORES + core})

    with jax.named_scope("start"):
        for k in range(1, ranks):
            stat_copy(k).start()
        for k in range(1, ranks):

            @pl.when(mine == k % particles)
            def _():
                w_copy(k).start()

        first.begin(first.pieces)
        first.keep()
        wbuf[me] = wt[me]

    def w_forward(k):
        q = k % particles

        @pl.when(mine == q)
        def _():
            w_arrived(k)
            for g in range(1, groups):
                w_to_group(k, g).start()
            w_to_core(k).start()

    def w_relay(k):
        q = k % particles

        @pl.when((core == q % CORES) & (grp != q // CORES))
        def _():
            w_arrived(k)
            w_to_core(k).start()

    def w_last(k):
        q = k % particles

        @pl.when(core != q % CORES)
        def _():
            w_arrived(k)

    with jax.named_scope("w1"):
        for k in range(1, ranks):
            w_forward(k)
    with jax.named_scope("g1a"):
        for t in range(1, near_half):
            first.step(t)
    with jax.named_scope("stats"):
        stat_all().wait_recv()
        by_group = jnp.sum(stats[...], axis=0) / count
        mean_g = by_group[0:1]
        inverse = lax.rsqrt(by_group[1:2] - mean_g * mean_g + 1e-05)
        back = jnp.concatenate([mean_g, inverse, jnp.zeros((6, LANES), f32)], axis=0)
        spread = jnp.dot(back, to_chan, precision=HIGH, preferred_element_type=f32)
        mean_c, inverse_c = spread[0:1], spread[1:2]
        loads[4].wait()
        loads[5].wait()
        gain = 1.0 + scale_ref[...].reshape(1, chans)
        bias = shift_ref[...].reshape(1, chans)

    def activate(slot):
        at = pl.ds(pl.multiple_of(slot * tokens, GRAIN), tokens)
        v = lat[at].astype(f32)
        v = (v - mean_c) * inverse_c * gain + bias
        act[at] = (v / (1.0 + jnp.exp(-v))).astype(bf16)

    half = total // 2
    mine_half = lax.div(a, near_half)

    def conv(which):
        at = pl.multiple_of(which * half, LANES)
        yt[:, pl.ds(at, half)] = lax.dot_general(
            wd[...], act[pl.ds(at, half)], NT, preferred_element_type=f32
        )

    with jax.named_scope("own"):
        activate(me)
    with jax.named_scope("g1b"):
        for t in range(near_half, outer - 1):
            first.step(t)
    with jax.named_scope("w2"):
        for k in range(1, ranks):
            w_relay(k)
    with jax.named_scope("act1"):
        first.rest(0)
        activate(other)
        for t in range(1, near_half):
            first.rest(t)
            each_slot(t, activate)
    with jax.named_scope("g1c"):
        first.step(outer - 1)
    with jax.named_scope("act2"):
        for t in range(near_half, outer - 1):
            first.rest(t)
            each_slot(t, activate)
    with jax.named_scope("w3"):
        for k in range(1, ranks):
            w_last(k)
    with jax.named_scope("wd"):
        line = jnp.concatenate([wbuf[r][:, :share] for r in range(ranks)], axis=1)
        for tap in range(TAPS):
            wd[tap * csp : (tap + 1) * csp] = line[:, tap * chans : (tap + 1) * chans]
    with jax.named_scope("conv1"):
        conv(mine_half)
    with jax.named_scope("act3"):
        first.rest(outer - 1)
        each_slot(outer - 1, activate)
    with jax.named_scope("conv2"):
        pick = lax.broadcasted_iota(jnp.int32, (csp, chans), 0)
        at = lax.broadcasted_iota(jnp.int32, (csp, chans), 1)
        pick = jnp.where((at == me * cs + pick) & (pick < cs), 1.0, 0.0).astype(bf16)
        field[...] = lax.dot_general(pick, lat[...], NT, preferred_element_type=f32)
        conv(1 - mine_half)

    with jax.named_scope("taps"):
        lane = lax.broadcasted_iota(jnp.int32, (1, total), 1)
        column = lax.rem(lane, width)
        has_left = column > 0
        has_right = column < width - 1
        has_above = lane >= width
        has_below = lane < total - width

        def add_taps(i, carry):
            def tap(row, col):
                base = (row * 3 + col) * csp
                return yt[pl.ds(pl.multiple_of(base + i * GRAIN, GRAIN), GRAIN), :]

            cols = []
            for col in range(3):
                above = jnp.where(has_above, pltpu.roll(tap(0, col), width, 1), 0.0)
                below = jnp.where(has_below, pltpu.roll(tap(2, col), total - width, 1), 0.0)
                cols.append(tap(1, col) + above + below)
            left = jnp.where(has_left, pltpu.roll(cols[0], 1, 1), 0.0)
            right = jnp.where(has_right, pltpu.roll(cols[2], total - 1, 1), 0.0)
            at = pl.ds(pl.multiple_of(i * GRAIN, GRAIN), GRAIN)
            chunk[at] = (field[at] + (cols[1] + left + right)).astype(bf16)
            return carry

        for i in second.pieces:
            start, size = second.cuts[i]
            lax.fori_loop(start // GRAIN, (start + size) // GRAIN, add_taps, 0)
            second.begin([i])
        second.keep()

    own_r = lax.broadcasted_iota(jnp.int32, (csp, csp), 0)
    own_c = lax.broadcasted_iota(jnp.int32, (csp, csp), 1)
    same = (lax.div(own_r, per_group) == lax.div(own_c, per_group)) & (own_r < cs) & (own_c < cs)
    same = jnp.where(same, 1.0, 0.0).astype(f32)
    lane = lax.broadcasted_iota(jnp.int32, (csp, LANES), 1)

    def normalize(slot):
        at = pl.ds(pl.multiple_of(slot * csp, GRAIN), csp)
        v = rt[at].astype(f32)
        both = jnp.where(
            lane == 0,
            jnp.sum(v, axis=1, keepdims=True),
            jnp.where(lane == 1, jnp.sum(v * v, axis=1, keepdims=True), 0.0),
        )
        both = jnp.dot(same, both, precision=HIGH, preferred_element_type=f32) / count
        mean = both[:, 0:1]
        inv = lax.rsqrt(both[:, 1:2] - mean * mean + 1e-05)
        nt[at] = ((v - mean) * inv).astype(bf16)

    with jax.named_scope("g2"):
        loads[1].wait()
        if cpad != chans:
            wqkv[...] = jnp.zeros_like(wqkv)
            for d in range(ranks):
                wqkv[d * csp : d * csp + cs] = wpad[d * cs : (d + 1) * cs]
        for n in range(2 * tiles):
            wkvt[n * LANES : (n + 1) * LANES] = wqkv[
                :, chans + n * LANES : chans + (n + 1) * LANES
            ].T
        normalize(me)
        for t in range(1, outer):
            second.step(t)
        second.rest(0)
        normalize(other)
        for t in range(1, outer):
            second.rest(t)
            each_slot(t, normalize)

    with jax.named_scope("qkv"):
        step = 2 * LANES
        for n in range(2 * chans // step):
            kvt[n * step : (n + 1) * step] = jnp.dot(
                wkvt[n * step : (n + 1) * step], nt[...], preferred_element_type=f32
            ).astype(bf16)
        row = lax.broadcasted_iota(jnp.int32, (tokens, total), 0)
        at = lax.broadcasted_iota(jnp.int32, (tokens, total), 1)
        pick = jnp.where(at == me * tokens + row, 1.0, 0.0).astype(bf16)
        mine_n = lax.dot_general(pick, nt[...], NT, preferred_element_type=f32).astype(bf16)
        resid = lax.dot_general(pick, rt[...], NT, preferred_element_type=f32)
        if cpad != chans:
            resid = jnp.concatenate(
                [resid[:, d * csp : d * csp + cs] for d in range(ranks)], axis=1
            )
        query = jnp.dot(mine_n, wqkv[:, :chans], preferred_element_type=f32).astype(bf16)

    with jax.named_scope("attn"):
        pair = 2 * head_dim
        lane = lax.broadcasted_iota(jnp.int32, (tokens, pair), 1)
        low = lane < head_dim
        zero = jnp.zeros((tokens, pair), bf16)
        for h in range(HEADS // 2):
            q = query[:, h * pair : (h + 1) * pair]
            q = jnp.concatenate([jnp.where(low, q, zero), jnp.where(low, zero, q)], axis=0)
            scores = jnp.dot(
                q, kvt[h * pair : (h + 1) * pair], preferred_element_type=f32
            ) * (head_dim ** (-0.5))
            top = jnp.max(scores, axis=1, keepdims=True)
            weights = jnp.exp(scores - top)
            norm = jnp.sum(weights, axis=1, keepdims=True)
            mixed = (
                lax.dot_general(
                    weights.astype(bf16),
                    kvt[chans + h * pair : chans + (h + 1) * pair],
                    NT,
                    preferred_element_type=f32,
                )
                / norm
            )
            att[:, h * pair : (h + 1) * pair] = jnp.where(
                low, mixed[:tokens], mixed[tokens:]
            ).astype(bf16)
    def to_core(p, j):
        where = {"particle": grp * CORES + (1 - core)}
        return remote(blocks.at[p, j], blocks.at[p, j], ps.at[0], pr.at[0, 0], where)

    def to_group(j, g):
        where = {"particle": lax.rem(grp + g, groups) * CORES + core}
        return remote(blocks.at[mine, j], blocks.at[mine, j], ps.at[g], pr.at[g, j], where)

    def from_group(j, g):
        part = blocks.at[of_group(g, core), j]
        remote(part, part, ps.at[g], pr.at[g, j], {"rows": other}).wait_recv()

    def whole_blocks(n, sem):
        part = blocks.at[0:n]
        return remote(part, part, ps.at[sem], pr.at[0, 0], {"rows": other})

    def of_group(g, side):
        return lax.rem(grp + groups - g, groups) * CORES + side

    with jax.named_scope("proj"):
        loads[2].wait()
        for j in range(tiles):
            at = slice(j * LANES, (j + 1) * LANES)
            blocks[mine, j] = (
                resid[:, at] + jnp.dot(att[...], wout[:, at], preferred_element_type=f32)
            ).astype(bf16)
            for g in range(1, groups):
                to_group(j, g).start()
            to_core(mine, j).start()

    with jax.named_scope("resample"):
        for j in range(tiles):
            for g in range(1, groups):
                from_group(j, g)
                to_core(of_group(g, core), j).start()
        whole_blocks(groups, 0).wait_recv()
        for j in range(tiles):
            out_ref[:, j * LANES : (j + 1) * LANES] = blocks[anc_ref[mine], j]
    with jax.named_scope("drain"):
        whole_blocks(groups, 0).wait_send()
        for g in range(1, groups):
            whole_blocks(1, g).wait_send()
        first.finish()
        second.finish()
        stat_all().wait_send()
        for q in range(particles):
            count = len(range(q, ranks, particles)) - (q == 0)

            @pl.when(mine == q)
            def _():
                part = wbuf.at[0:count]
                for g in [0] + list(range(2, groups + 1)):
                    remote(part, part, ws.at[g], wr.at[0], {"rows": other}).wait_send()

        for c in range(CORES):
            count = sum(k % particles % CORES == c for k in range(1, ranks))

            @pl.when(core == c)
            def _():
                part = wbuf.at[0:count]
                remote(part, part, ws.at[1], wr.at[0], {"rows": other}).wait_send()


def per_device(latent, ada_scale, ada_shift, conv_weight, qkv_weight, out_weight, ancestors):
    _, rows_here, width, chans = latent.shape
    tokens = rows_here * width
    ranks = lax.axis_size("rows")
    particles = lax.axis_size("particle")
    groups = particles // CORES
    total = tokens * ranks
    share = conv_weight.shape[0]
    span = -(-share // LANES) * LANES
    if share % GRAIN:
        conv_weight = jnp.pad(conv_weight, ((0, span - share), (0, 0)))
    cs = chans // ranks
    csp = -(-cs // GRAIN) * GRAIN
    cpad = csp * ranks
    outer = ranks // INNER
    n1, n2 = len(cut_rows(tokens, CUT1)), len(cut_rows(csp, CUT2))
    dims = (rows_here, width, chans, ranks, particles, share)
    bf16, f32 = jnp.bfloat16, jnp.float32
    dma = pltpu.SemaphoreType.DMA
    out = pl.pallas_call(
        functools.partial(kernel, dims),
        out_shape=jax.ShapeDtypeStruct((tokens, chans), bf16),
        in_specs=[pl.BlockSpec(memory_space=pltpu.SMEM)]
        + [pl.BlockSpec(memory_space=pl.ANY)] * 6,
        out_specs=pl.BlockSpec(memory_space=pltpu.VMEM),
        scratch_shapes=[
            pltpu.VMEM((tokens, chans), bf16),
            pltpu.VMEM(ada_scale.shape, f32),
            pltpu.VMEM(ada_shift.shape, f32),
            pltpu.VMEM((span, chans), bf16),
            pltpu.VMEM((ranks, csp, span), bf16),
            pltpu.VMEM((ranks, csp, span), bf16),
            pltpu.VMEM((TAPS * csp, chans), bf16),
            pltpu.VMEM((cpad, 3 * chans), bf16),
            pltpu.VMEM((GRAIN, LANES) if cpad == chans else qkv_weight.shape, bf16),
            pltpu.VMEM((2 * chans, cpad), bf16),
            pltpu.VMEM(out_weight.shape, bf16),
            pltpu.VMEM((total, chans), bf16),
            pltpu.VMEM((total, chans), bf16),
            pltpu.VMEM((TAPS * csp, total), f32),
            pltpu.VMEM((csp, total), f32),
            pltpu.VMEM((csp, total), bf16),
            pltpu.VMEM((cpad, total), bf16),
            pltpu.VMEM((cpad, total), bf16),
            pltpu.VMEM((2 * chans, total), bf16),
            pltpu.VMEM((tokens, chans), bf16),
            pltpu.VMEM((particles, chans // LANES, tokens, LANES), bf16),
            pltpu.VMEM((8, LANES), f32),
            pltpu.VMEM((ranks, 8, LANES), f32),
            dma((6,)),
            dma((1 + groups,)),
            dma((ranks,)),
            dma((2,)),
            dma((3,)),
            dma((outer, n1)),
            dma((outer,)),
            dma((3,)),
            dma((outer, n2)),
            dma((outer,)),
            dma((groups,)),
            dma((groups, chans // LANES)),
        ],
        compiler_params=pltpu.CompilerParams(
            collective_id=0, has_side_effects=True, vmem_limit_bytes=64000 * 1024
        ),
        name="block",
    )(
        ancestors,
        latent.reshape(tokens, chans),
        ada_scale,
        ada_shift,
        conv_weight,
        qkv_weight,
        out_weight,
    )
    return out.reshape(latent.shape)


def solution(mesh):
    in_specs = (P("particle", "rows", None, None), P(), P(), P("rows", None), P(), P(), P())
    out_specs = P("particle", "rows", None, None)
    return jax.shard_map(
        per_device, mesh=mesh, in_specs=in_specs, out_specs=out_specs, check_vma=False
    )
```

```python
import functools
import math

import jax
import jax.numpy as jnp
from jax import lax
from jax.experimental import pallas as pl
from jax.experimental.pallas import tpu as pltpu
from jax.sharding import PartitionSpec as P

HEADS = 10
GROUPS = 32
INNER = 2
CUT1 = 2
CUT2 = 1
HOP1 = 0
HOP2 = 0
STRAIGHT = 2
WIDE = 2
DIRECT2 = 0
CORES = 2
LANES = 128
GRAIN = 16
TAPS = 9
MESH = pl.DeviceIdType.MESH
NT = (((1,), (1,)), ((), ()))
HIGH = lax.Precision.HIGHEST


def cut_rows(rows, grains):
    step = grains * GRAIN
    return [(at, min(step, rows - at)) for at in range(0, rows, step)]


def kernel(
    dims,
    anc_ref,
    x_hbm,
    scale_hbm,
    shift_hbm,
    wconv_hbm,
    wqkv_hbm,
    wout_hbm,
    out_ref,
    x_ref,
    scale_ref,
    shift_ref,
    wz,
    wt,
    wbuf,
    wd,
    wqkv,
    wpad,
    wnear,
    wmid,
    wlate,
    kacc,
    wout,
    lat,
    act,
    yt,
    field,
    chunk,
    rt,
    nt,
    kvt,
    att,
    blocks,
    stat_own,
    stats,
    norm_own,
    norms,
    load_sem,
    ns,
    nr,
    ws,
    wr,
    ss,
    sent1,
    near1,
    far1,
    turned1,
    side1,
    sent2,
    near2,
    far2,
    turned2,
    side2,
    ps,
    pr,
):
    rows_here, width, chans, ranks, particles, share, early = dims
    tokens = rows_here * width
    total = tokens * ranks
    outer = ranks // INNER
    groups = particles // CORES
    cs = chans // ranks
    csp = chunk.shape[0]
    cpad = ranks * csp
    per_group = chans // GROUPS
    count = total * per_group
    head_dim = chans // HEADS
    tiles = chans // LANES
    bf16, f32 = jnp.bfloat16, jnp.float32
    me = lax.axis_index("rows")
    mine = lax.axis_index("particle")
    a = lax.div(me, INNER)
    b = lax.rem(me, INNER)
    other = a * INNER + (1 - b)
    grp = lax.div(mine, CORES)
    core = lax.rem(mine, CORES)

    conv_in = wz.at[0 : wconv_hbm.shape[0]]
    qkv_in = wqkv if cpad == chans else wpad
    loads = [
        pltpu.make_async_copy(wconv_hbm, conv_in, load_sem.at[0]),
        pltpu.make_async_copy(wqkv_hbm, qkv_in, load_sem.at[1]),
        pltpu.make_async_copy(wout_hbm, wout, load_sem.at[2]),
        pltpu.make_async_copy(x_hbm, x_ref, load_sem.at[3]),
        pltpu.make_async_copy(scale_hbm, scale_ref, load_sem.at[4]),
        pltpu.make_async_copy(shift_hbm, shift_ref, load_sem.at[5]),
    ]
    for i in (3, 0, 4, 5, 1, 2):
        loads[i].start()

    barrier = pltpu.get_barrier_semaphore()
    for k in range(1, ranks):
        pl.semaphore_signal(
            barrier, inc=1, device_id={"rows": lax.rem(me + k, ranks)}, device_id_type=MESH
        )
    for k in range(1, particles):
        pl.semaphore_signal(
            barrier,
            inc=1,
            device_id={"particle": lax.rem(mine + k, particles)},
            device_id_type=MESH,
        )

    if wz.shape[0] > wconv_hbm.shape[0]:
        tail = wz.shape[0] - wconv_hbm.shape[0]
        wz[wconv_hbm.shape[0] :] = jnp.zeros((tail, chans), bf16)

    chan_r = lax.broadcasted_iota(jnp.int32, (chans, LANES), 0)
    group_r = lax.broadcasted_iota(jnp.int32, (chans, LANES), 1) * per_group
    inside = (chan_r >= group_r) & (chan_r < group_r + per_group)
    to_group = jnp.where(inside, 1.0, 0.0).astype(f32)
    group_c = lax.broadcasted_iota(jnp.int32, (LANES, chans), 0) * per_group
    chan_c = lax.broadcasted_iota(jnp.int32, (LANES, chans), 1)
    inside = (chan_c >= group_c) & (chan_c < group_c + per_group)
    to_chan = jnp.where(inside, 1.0, 0.0).astype(f32)

    loads[3].wait()
    x32 = x_ref[...].astype(f32)
    sums = jnp.concatenate(
        [
            jnp.sum(x32, axis=0, keepdims=True),
            jnp.sum(x32 * x32, axis=0, keepdims=True),
            jnp.zeros((6, chans), f32),
        ],
        axis=0,
    )
    stat_own[...] = jnp.dot(sums, to_group, precision=HIGH, preferred_element_type=f32)
    stats[me] = stat_own[...]

    with jax.named_scope("turn"):
        loads[0].wait()
        turned = wz[...].T
        for d in range(ranks):
            wt[d, 0:cs] = turned[d * cs : (d + 1) * cs]
            if csp != cs:
                wt[d, cs:csp] = jnp.zeros((csp - cs, wt.shape[2]), bf16)

    with jax.named_scope("barrier"):
        pl.semaphore_wait(barrier, ranks + particles - 2)

    def remote(src, dst, send, recv, where):
        return pltpu.make_async_remote_copy(
            src_ref=src,
            dst_ref=dst,
            send_sem=send,
            recv_sem=recv,
            device_id=where,
            device_id_type=MESH,
        )

    class Gather:
        def __init__(self, src, buf, rows, cuts, hop, sent, near, far, turned, side_far):
            self.src, self.buf, self.rows, self.cuts = src, buf, rows, cuts
            self.sent, self.near, self.far = sent, near, far
            self.turned, self.side_far = turned, side_far
            self.hop = hop
            self.hop_rows = cuts[hop][0]
            self.pieces = range(len(cuts))

        def rows_of(self, slot, start, size):
            return self.buf.at[pl.ds(pl.multiple_of(slot * self.rows + start, GRAIN), size)]

        def send(self, slot, i, side, recv, own=False):
            start, size = self.cuts[i]
            dst = self.rows_of(slot, start, size)
            src = self.src.at[pl.ds(start, size)] if own else dst
            row = (a + side) * INNER + b if side else other
            return remote(src, dst, self.sent.at[side + 1], recv, {"rows": row})

        def along(self, origin, i, side, own=False):
            return self.send(origin * INNER + b, i, side, self.near.at[origin, i], own)

        def across(self, origin, i, own=False):
            recv = self.turned.at[i] if own and i < self.hop else self.far.at[origin]
            return self.send(origin * INNER + b, i, 0, recv, own)

        def begin(self, pieces):
            for i in pieces:
                self.across(a, i, True).start()
                for side, onward in ((1, a + 1 < outer), (-1, a > 0)):

                    @pl.when(onward)
                    def _():
                        self.along(a, i, side, True).start()

        def keep(self):
            self.buf[pl.ds(pl.multiple_of(me * self.rows, GRAIN), self.rows)] = self.src[...]

        def turn(self):
            for i in range(self.hop):
                self.send(other, i, 0, self.turned.at[i]).wait_recv()
                for side, onward in ((1, a + 1 < outer), (-1, a > 0)):

                    @pl.when(onward)
                    def _():
                        self.send(other, i, side, self.side_far.at[(1 + side) // 2]).start()

        def sides(self, t):
            return ((a >= t, a - t, 1, a + 1 < outer), (a + t < outer, a + t, -1, a > 0))

        def order(self, t):
            return list(self.pieces)

        def step(self, t, pieces=None):
            for i in self.pieces if pieces is None else pieces:
                for present, origin, side, onward in self.sides(t):

                    @pl.when(present)
                    def _():
                        self.along(origin, i, 1).wait_recv()

                        @pl.when(onward)
                        def _():
                            self.along(origin, i, side).start()

                        if t > 1 or i >= self.hop:
                            self.across(origin, i).start()

        def got(self, slot, start, size, recv):
            part = self.rows_of(slot, start, size)
            remote(part, part, self.sent.at[1], recv, {"rows": other}).wait_recv()

        def rest(self, t):
            if t == 0:
                self.got(other, self.hop_rows, self.rows - self.hop_rows, self.far.at[a])
                return
            for present, origin, side, _ in self.sides(t):
                slot = origin * INNER + (1 - b)

                @pl.when(present)
                def _():
                    if t > 1 or not self.hop:
                        self.got(slot, 0, self.rows, self.far.at[origin])
                    else:
                        top = self.hop_rows
                        self.got(slot, 0, top, self.side_far.at[(1 + side) // 2])
                        self.got(slot, top, self.rows - top, self.far.at[origin])

        def sent_all(self, side, rows):
            part = self.buf.at[0:rows]
            remote(part, part, self.sent.at[side + 1], self.far.at[0], {"rows": other}).wait_send()

        def finish(self):
            for v in range(outer):

                @pl.when(a == v)
                def _():
                    beside = (v > 0) + (v + 1 < outer)
                    self.sent_all(0, outer * self.rows - beside * self.hop_rows)
                    if v + 1 < outer:
                        self.sent_all(1, (v + 1) * self.rows + self.hop_rows)
                    if v > 0:
                        self.sent_all(-1, (outer - v) * self.rows + self.hop_rows)

    def each_of(t, column, fn):
        if t == 0:
            fn(a * INNER + column)
            return
        for present, origin in ((a >= t, a - t), (a + t < outer, a + t)):

            @pl.when(present)
            def _():
                fn(origin * INNER + column)

    def each_near(t, fn):
        each_of(t, b, fn)

    def each_far(t, fn):
        each_of(t, 1 - b, fn)

    def each_slot(t, fn):
        if t == 0:
            fn(me)
            fn(other)
            return
        for present, origin in ((a >= t, a - t), (a + t < outer, a + t)):

            @pl.when(present)
            def _():
                fn(origin * INNER + b)
                fn(origin * INNER + (1 - b))

    near_half = outer // 2
    hop2 = min(HOP2, csp // (CUT2 * GRAIN) - 1)
    first = Gather(x_ref, lat, tokens, cut_rows(tokens, CUT1), HOP1, sent1, near1, far1, turned1, side1)
    second = Gather(chunk, rt, csp, cut_rows(csp, CUT2), hop2, sent2, near2, far2, turned2, side2)

    def stat_copy(k):
        return remote(
            stat_own, stats.at[me], ss.at[0], ss.at[1], {"rows": lax.rem(me + k, ranks)}
        )

    def stat_all():
        part = stats.at[0 : ranks - 1]
        return remote(part, part, ss.at[0], ss.at[1], {"rows": other})

    def w_copy(k):
        dest = lax.rem(me + k, ranks)
        return remote(wt.at[dest], wbuf.at[me], ws.at[0], wr.at[me], {"rows": dest})

    def w_slot(k):
        return lax.rem(me + ranks - k, ranks)

    def w_pass_on(k, j, where):
        slot = w_slot(k)
        return remote(wbuf.at[slot], wbuf.at[slot], ws.at[j], wr.at[slot], where)

    def w_arrived(k):
        w_pass_on(k, 1, {"rows": other}).wait_recv()

    def w_to_core(k):
        return w_pass_on(k, 1, {"particle": grp * CORES + (1 - core)})

    def w_to_group(k, g):
        return w_pass_on(k, 1 + g, {"particle": lax.rem(grp + g, groups) * CORES + core})

    with jax.named_scope("start"):
        for k in range(1, ranks):
            stat_copy(k).start()
        for k in range(particles, ranks):

            @pl.when(mine == k % particles)
            def _():
                w_copy(k).start()

        first.begin(first.pieces)
        for k in range(1, particles):

            @pl.when(mine == k % particles)
            def _():
                w_copy(k).start()

        first.keep()
        wbuf[me] = wt[me]

    def w_forward(k):
        q = k % particles

        @pl.when(mine == q)
        def _():
            w_arrived(k)
            for g in range(1, groups):
                w_to_group(k, g).start()
            w_to_core(k).start()

    def w_relay(k):
        q = k % particles

        @pl.when((core == q % CORES) & (grp != q // CORES))
        def _():
            w_arrived(k)
            w_to_core(k).start()

    def w_last(k):
        q = k % particles

        @pl.when(core != q % CORES)
        def _():
            w_arrived(k)

    low_end = a < near_half
    with jax.named_scope("kvw"):
        loads[1].wait()
        if cpad != chans:
            wqkv[...] = jnp.zeros_like(wqkv)
            for d in range(ranks):
                wqkv[d * csp : d * csp + cs] = wpad[d * cs : (d + 1) * cs]
        late = INNER * csp
        near_size = cpad // 2
        parts = (
            (jnp.where(low_end, 0, near_size), near_size, wnear),
            (jnp.where(low_end, near_size, late), near_size - late, wmid),
            (jnp.where(low_end, cpad - late, 0), late, wlate),
        )
        parts = [(pl.multiple_of(at, GRAIN), size, dst) for at, size, dst in parts]
        for at, size, dst in parts:
            for n in range(2 * tiles):
                dst[n * LANES : (n + 1) * LANES] = wqkv[
                    pl.ds(at, size), chans + n * LANES : chans + (n + 1) * LANES
                ].T
    with jax.named_scope("g1a"):
        for t in range(1, near_half):
            first.step(t)
    with jax.named_scope("stats"):
        stat_all().wait_recv()
        by_group = jnp.sum(stats[...], axis=0) / count
        mean_g = by_group[0:1]
        inverse = lax.rsqrt(by_group[1:2] - mean_g * mean_g + 1e-05)
        back = jnp.concatenate([mean_g, inverse, jnp.zeros((6, LANES), f32)], axis=0)
        spread = jnp.dot(back, to_chan, precision=HIGH, preferred_element_type=f32)
        mean_c, inverse_c = spread[0:1], spread[1:2]
        loads[4].wait()
        loads[5].wait()
        gain = 1.0 + scale_ref[...].reshape(1, chans)
        bias = shift_ref[...].reshape(1, chans)

    def activate(slot):
        at = pl.ds(pl.multiple_of(slot * tokens, GRAIN), tokens)
        v = lat[at].astype(f32)
        v = (v - mean_c) * inverse_c * gain + bias
        act[at] = (v / (1.0 + jnp.exp(-v))).astype(bf16)

    half = total // 2
    mine_half = lax.div(a, near_half)

    def conv(which):
        at = pl.multiple_of(which * half, LANES)
        yt[:, pl.ds(at, half)] = lax.dot_general(
            wd[...], act[pl.ds(at, half)], NT, preferred_element_type=f32
        )

    with jax.named_scope("wf2"):
        for k in range(particles, ranks):
            w_forward(k)
    with jax.named_scope("own"):
        activate(me)
    with jax.named_scope("g1b0"):
        for t in range(near_half, outer - 1):
            first.step(t, first.order(t)[:1])
    with jax.named_scope("wf1"):
        for k in range(1, min(particles, ranks)):
            w_forward(k)
    with jax.named_scope("g1b1"):
        for t in range(near_half, outer - 1):
            first.step(t, first.order(t)[1:])
    with jax.named_scope("act1"):
        first.rest(0)
        activate(other)
        for t in range(1, near_half):
            first.rest(t)
            each_slot(t, activate)
    with jax.named_scope("g1c"):
        first.step(outer - 1)
    with jax.named_scope("w2"):
        for k in range(1, ranks):
            w_relay(k)
    with jax.named_scope("act2"):
        for t in range(near_half, outer - 1):
            first.rest(t)
            each_slot(t, activate)
    with jax.named_scope("w3"):
        for k in range(1, ranks):
            w_last(k)
    with jax.named_scope("wd"):
        line = jnp.concatenate([wbuf[r][:, :share] for r in range(ranks)], axis=1)
        for tap in range(TAPS):
            wd[tap * csp : (tap + 1) * csp] = line[:, tap * chans : (tap + 1) * chans]
    with jax.named_scope("conv1"):
        conv(mine_half)
    with jax.named_scope("act3"):
        first.rest(outer - 1)
        each_slot(outer - 1, activate)
    with jax.named_scope("conv2"):
        pick = lax.broadcasted_iota(jnp.int32, (csp, chans), 0)
        at = lax.broadcasted_iota(jnp.int32, (csp, chans), 1)
        pick = jnp.where((at == me * cs + pick) & (pick < cs), 1.0, 0.0).astype(bf16)
        field[...] = lax.dot_general(pick, lat[...], NT, preferred_element_type=f32)
        conv(1 - mine_half)

    with jax.named_scope("taps"):
        lane = lax.broadcasted_iota(jnp.int32, (1, total), 1)
        column = lax.rem(lane, width)
        has_left = column > 0
        has_right = column < width - 1
        has_above = lane >= width
        has_below = lane < total - width

        def add_taps(i, carry):
            def tap(row, col):
                base = (row * 3 + col) * csp
                return yt[pl.ds(pl.multiple_of(base + i * GRAIN, GRAIN), GRAIN), :]

            cols = []
            for col in range(3):
                above = jnp.where(has_above, pltpu.roll(tap(0, col), width, 1), 0.0)
                below = jnp.where(has_below, pltpu.roll(tap(2, col), total - width, 1), 0.0)
                cols.append(tap(1, col) + above + below)
            left = jnp.where(has_left, pltpu.roll(cols[0], 1, 1), 0.0)
            right = jnp.where(has_right, pltpu.roll(cols[2], total - 1, 1), 0.0)
            at = pl.ds(pl.multiple_of(i * GRAIN, GRAIN), GRAIN)
            chunk[at] = (field[at] + (cols[1] + left + right)).astype(bf16)
            return carry

        for i in second.pieces:
            start, size = second.cuts[i]
            lax.fori_loop(start // GRAIN, (start + size) // GRAIN, add_taps, 0)
            second.begin([i])
        second.keep()

    own_r = lax.broadcasted_iota(jnp.int32, (csp, csp), 0)
    own_c = lax.broadcasted_iota(jnp.int32, (csp, csp), 1)
    same = (lax.div(own_r, per_group) == lax.div(own_c, per_group)) & (own_r < cs) & (own_c < cs)
    same = jnp.where(same, 1.0, 0.0).astype(f32)
    lane = lax.broadcasted_iota(jnp.int32, (csp, LANES), 1)

    def norm_copy(k):
        return remote(
            norm_own, norms.at[me], ns.at[0], nr.at[me], {"rows": lax.rem(me + k, ranks)}
        )

    with jax.named_scope("own"):
        v = chunk[...].astype(f32)
        both = jnp.where(
            lane == 0,
            jnp.sum(v, axis=1, keepdims=True),
            jnp.where(lane == 1, jnp.sum(v * v, axis=1, keepdims=True), 0.0),
        )
        both = jnp.dot(same, both, precision=HIGH, preferred_element_type=f32) / count
        mean = both[:, 0:1]
        inv = lax.rsqrt(both[:, 1:2] - mean * mean + 1e-05)
        both = jnp.where(lane == 0, mean, jnp.where(lane == 1, inv, 0.0))
        both = jnp.concatenate([both, jnp.zeros((LANES - csp, LANES), f32)], axis=0)
        norm_own[...] = both.T[0:8]
        for k in range(1, ranks):
            norm_copy(k).start()
        nt[pl.ds(pl.multiple_of(me * csp, GRAIN), csp)] = ((v - mean) * inv).astype(bf16)

    def normalize(slot):
        at = pl.ds(pl.multiple_of(slot * csp, GRAIN), csp)
        remote(norm_own, norms.at[slot], ns.at[0], nr.at[slot], {"rows": other}).wait_recv()
        both = norms[slot].T
        v = rt[at].astype(f32)
        nt[at] = ((v - both[:csp, 0:1]) * both[:csp, 1:2]).astype(bf16)

    step = 2 * LANES
    kv_rows = [slice(n * step, (n + 1) * step) for n in range(2 * chans // step)]

    def kv_part(i, rows):
        at, size, weights = parts[i]
        return jnp.dot(weights[rows], nt[pl.ds(at, size)], preferred_element_type=f32)

    with jax.named_scope("g2"):
        for t in range(1, outer):
            second.step(t)
            second.rest(t - 1)
            each_far(t - 1, normalize)
            each_near(t, normalize)
            if early and t == near_half:
                for rows in kv_rows:
                    kacc[rows] = kv_part(0, rows)

    with jax.named_scope("kv1"):
        row = lax.broadcasted_iota(jnp.int32, (tokens, total), 0)
        at = lax.broadcasted_iota(jnp.int32, (tokens, total), 1)
        pick = jnp.where(at == me * tokens + row, 1.0, 0.0).astype(bf16)

        def query_part(i):
            at, size, _ = parts[i]
            at = pl.ds(at, size)
            own = lax.dot_general(pick, nt[at], NT, preferred_element_type=f32).astype(bf16)
            return jnp.dot(own, wqkv[at, :chans], preferred_element_type=f32)

        query = query_part(0) + query_part(1)
        if early:
            for rows in kv_rows:
                kacc[rows] += kv_part(1, rows)
    with jax.named_scope("g2b"):
        second.rest(outer - 1)
        each_far(outer - 1, normalize)

    with jax.named_scope("qkv"):
        query = (query + query_part(2)).astype(bf16)
        for rows in kv_rows:
            head = kacc[rows] if early else kv_part(0, rows) + kv_part(1, rows)
            kvt[rows] = (head + kv_part(2, rows)).astype(bf16)
        resid = lax.dot_general(pick, rt[...], NT, preferred_element_type=f32)
        if cpad != chans:
            resid = jnp.concatenate(
                [resid[:, d * csp : d * csp + cs] for d in range(ranks)], axis=1
            )

    with jax.named_scope("attn"):
        pair = 2 * head_dim
        lane = lax.broadcasted_iota(jnp.int32, (tokens, pair), 1)
        low = lane < head_dim
        zero = jnp.zeros((tokens, pair), bf16)
        for h in range(HEADS // 2):
            q = query[:, h * pair : (h + 1) * pair]
            q = jnp.concatenate([jnp.where(low, q, zero), jnp.where(low, zero, q)], axis=0)
            scores = jnp.dot(
                q, kvt[h * pair : (h + 1) * pair], preferred_element_type=f32
            ) * (head_dim ** (-0.5))
            top = jnp.max(scores, axis=1, keepdims=True)
            weights = jnp.exp(scores - top)
            norm = jnp.sum(weights, axis=1, keepdims=True)
            mixed = (
                lax.dot_general(
                    weights.astype(bf16),
                    kvt[chans + h * pair : chans + (h + 1) * pair],
                    NT,
                    preferred_element_type=f32,
                )
                / norm
            )
            att[:, h * pair : (h + 1) * pair] = jnp.where(
                low, mixed[:tokens], mixed[tokens:]
            ).astype(bf16)
    def to_core(p, j):
        where = {"particle": grp * CORES + (1 - core)}
        return remote(blocks.at[p * tiles + j], blocks.at[p * tiles + j], ps.at[0], pr.at[0, 0], where)

    def to_group(j, g, cross=0):
        there = 1 - core if cross else core
        where = {"particle": lax.rem(grp + g, groups) * CORES + there}
        recv = pr.at[0, 1] if cross else pr.at[g, j]
        return remote(blocks.at[mine * tiles + j], blocks.at[mine * tiles + j], ps.at[groups if cross else g], recv, where)

    def from_group(j, g):
        part = blocks.at[of_group(g, core) * tiles + j]
        remote(part, part, ps.at[g], pr.at[g, j], {"rows": other}).wait_recv()

    def tiles_of(n, sem, recv=0):
        part = blocks.at[0:n]
        return remote(part, part, ps.at[sem], pr.at[0, recv], {"rows": other})

    passed = max(0, tiles - STRAIGHT)
    by_core = tiles + (groups - 1) * passed
    crossing = (groups - 1) * (tiles - passed)

    def of_group(g, side):
        return lax.rem(grp + groups - g, groups) * CORES + side

    with jax.named_scope("proj"):
        loads[2].wait()
        for j in range(tiles):
            if j % WIDE == 0:
                at = slice(j * LANES, min(j + WIDE, tiles) * LANES)
                wide = resid[:, at] + jnp.dot(
                    att[...], wout[:, at], preferred_element_type=f32
                )
            at = j % WIDE * LANES
            blocks[mine * tiles + j] = wide[:, at : at + LANES].astype(bf16)
            for g in range(1, groups):
                to_group(j, g).start()
            to_core(mine, j).start()
        for j in range(passed, tiles):
            for g in range(1, groups):
                to_group(j, g, 1).start()

    with jax.named_scope("resample"):
        for j in range(tiles):
            for g in range(1, groups):
                from_group(j, g)
                if j < passed:
                    to_core(of_group(g, core), j).start()
        tiles_of(by_core, 0).wait_recv()
        if crossing:
            tiles_of(crossing, 0, 1).wait_recv()
        for j in range(tiles):
            out_ref[:, j * LANES : (j + 1) * LANES] = blocks[anc_ref[mine] * tiles + j]
    with jax.named_scope("drain"):
        tiles_of(by_core, 0).wait_send()
        for g in range(1, groups):
            tiles_of(tiles, g).wait_send()
        if crossing:
            tiles_of(crossing, groups).wait_send()
        first.finish()
        second.finish()
        stat_all().wait_send()
        part = norms.at[0 : ranks - 1]
        remote(part, part, ns.at[0], nr.at[0], {"rows": other}).wait_send()
        for q in range(particles):
            count = len(range(q, ranks, particles)) - (q == 0)

            @pl.when(mine == q)
            def _():
                part = wbuf.at[0:count]
                for g in [0] + list(range(2, groups + 1)):
                    remote(part, part, ws.at[g], wr.at[0], {"rows": other}).wait_send()

        for c in range(CORES):
            count = sum(k % particles % CORES == c for k in range(1, ranks))

            @pl.when(core == c)
            def _():
                part = wbuf.at[0:count]
                remote(part, part, ws.at[1], wr.at[0], {"rows": other}).wait_send()


def per_device(latent, ada_scale, ada_shift, conv_weight, qkv_weight, out_weight, ancestors):
    _, rows_here, width, chans = latent.shape
    tokens = rows_here * width
    ranks = lax.axis_size("rows")
    particles = lax.axis_size("particle")
    groups = particles // CORES
    total = tokens * ranks
    share = conv_weight.shape[0]
    span = -(-share // LANES) * LANES
    if share % GRAIN:
        conv_weight = jnp.pad(conv_weight, ((0, span - share), (0, 0)))
    cs = chans // ranks
    csp = -(-cs // GRAIN) * GRAIN
    cpad = csp * ranks
    outer = ranks // INNER
    n1, n2 = len(cut_rows(tokens, CUT1)), len(cut_rows(csp, CUT2))
    early = outer <= 4
    dims = (rows_here, width, chans, ranks, particles, share, early)
    bf16, f32 = jnp.bfloat16, jnp.float32
    dma = pltpu.SemaphoreType.DMA
    out = pl.pallas_call(
        functools.partial(kernel, dims),
        out_shape=jax.ShapeDtypeStruct((tokens, chans), bf16),
        in_specs=[pl.BlockSpec(memory_space=pltpu.SMEM)]
        + [pl.BlockSpec(memory_space=pl.ANY)] * 6,
        out_specs=pl.BlockSpec(memory_space=pltpu.VMEM),
        scratch_shapes=[
            pltpu.VMEM((tokens, chans), bf16),
            pltpu.VMEM(ada_scale.shape, f32),
            pltpu.VMEM(ada_shift.shape, f32),
            pltpu.VMEM((span, chans), bf16),
            pltpu.VMEM((ranks, csp, span), bf16),
            pltpu.VMEM((ranks, csp, span), bf16),
            pltpu.VMEM((TAPS * csp, chans), bf16),
            pltpu.VMEM((cpad, 3 * chans), bf16),
            pltpu.VMEM((GRAIN, LANES) if cpad == chans else qkv_weight.shape, bf16),
            pltpu.VMEM((2 * chans, cpad // 2), bf16),
            pltpu.VMEM((2 * chans, cpad // 2 - INNER * csp), bf16),
            pltpu.VMEM((2 * chans, INNER * csp), bf16),
            pltpu.VMEM((2 * chans, total) if early else (8, LANES), f32),
            pltpu.VMEM(out_weight.shape, bf16),
            pltpu.VMEM((total, chans), bf16),
            pltpu.VMEM((total, chans), bf16),
            pltpu.VMEM((TAPS * csp, total), f32),
            pltpu.VMEM((csp, total), f32),
            pltpu.VMEM((csp, total), bf16),
            pltpu.VMEM((cpad, total), bf16),
            pltpu.VMEM((cpad, total), bf16),
            pltpu.VMEM((2 * chans, total), bf16),
            pltpu.VMEM((tokens, chans), bf16),
            pltpu.VMEM((particles * (chans // LANES), tokens, LANES), bf16),
            pltpu.VMEM((8, LANES), f32),
            pltpu.VMEM((ranks, 8, LANES), f32),
            pltpu.VMEM((8, LANES), f32),
            pltpu.VMEM((ranks, 8, LANES), f32),
            dma((6,)),
            dma((1,)),
            dma((ranks,)),
            dma((1 + groups,)),
            dma((ranks,)),
            dma((2,)),
            dma((3,)),
            dma((outer, n1)),
            dma((outer,)),
            dma((max(1, HOP1),)),
            dma((2,)),
            dma((3,)),
            dma((outer, n2)),
            dma((outer,)),
            dma((max(1, HOP2),)),
            dma((2,)),
            dma((groups + 1,)),
            dma((groups, chans // LANES)),
        ],
        compiler_params=pltpu.CompilerParams(
            collective_id=0, has_side_effects=True, vmem_limit_bytes=64000 * 1024
        ),
        name="block",
    )(
        ancestors,
        latent.reshape(tokens, chans),
        ada_scale,
        ada_shift,
        conv_weight,
        qkv_weight,
        out_weight,
    )
    return out.reshape(latent.shape)


def solution(mesh):
    in_specs = (P("particle", "rows", None, None), P(), P(), P("rows", None), P(), P(), P())
    out_specs = P("particle", "rows", None, None)
    return jax.shard_map(
        per_device, mesh=mesh, in_specs=in_specs, out_specs=out_specs, check_vma=False
    )
```

```python
import functools
import math

import jax
import jax.numpy as jnp
from jax import lax
from jax.experimental import pallas as pl
from jax.experimental.pallas import tpu as pltpu
from jax.sharding import PartitionSpec as P

HEADS = 10
GROUPS = 32
INNER = 2
CUT1 = 2
CUT2 = 1
STRAIGHT = 2
WIDE = 2
DIRECT2 = 0
CORES = 2
LANES = 128
GRAIN = 16
TAPS = 9
MESH = pl.DeviceIdType.MESH
NT = (((1,), (1,)), ((), ()))
HIGH = lax.Precision.HIGHEST


def cut_rows(rows, grains):
    step = grains * GRAIN
    return [(at, min(step, rows - at)) for at in range(0, rows, step)]


def kernel(
    dims,
    anc_ref,
    x_hbm,
    scale_hbm,
    shift_hbm,
    wconv_hbm,
    wqkv_hbm,
    wout_hbm,
    out_ref,
    x_ref,
    scale_ref,
    shift_ref,
    wz,
    wt,
    wbuf,
    wd,
    wqkv,
    wpad,
    wnear,
    wmid,
    wlate,
    kacc,
    wout,
    lat,
    act,
    yt,
    field,
    chunk,
    rt,
    nt,
    kvt,
    att,
    blocks,
    stat_own,
    stats,
    norm_own,
    norms,
    load_sem,
    ns,
    nr,
    ws,
    wr,
    ss,
    sent1,
    near1,
    far1,
    sent2,
    near2,
    far2,
    ps,
    pr,
):
    rows_here, width, chans, ranks, particles, share, early = dims
    tokens = rows_here * width
    total = tokens * ranks
    outer = ranks // INNER
    groups = particles // CORES
    cs = chans // ranks
    csp = chunk.shape[0]
    cpad = ranks * csp
    per_group = chans // GROUPS
    count = total * per_group
    head_dim = chans // HEADS
    tiles = chans // LANES
    bf16, f32 = jnp.bfloat16, jnp.float32
    me = lax.axis_index("rows")
    mine = lax.axis_index("particle")
    a = lax.div(me, INNER)
    b = lax.rem(me, INNER)
    other = a * INNER + (1 - b)
    grp = lax.div(mine, CORES)
    core = lax.rem(mine, CORES)

    conv_in = wz.at[0 : wconv_hbm.shape[0]]
    qkv_in = wqkv if cpad == chans else wpad
    loads = [
        pltpu.make_async_copy(wconv_hbm, conv_in, load_sem.at[0]),
        pltpu.make_async_copy(wqkv_hbm, qkv_in, load_sem.at[1]),
        pltpu.make_async_copy(wout_hbm, wout, load_sem.at[2]),
        pltpu.make_async_copy(x_hbm, x_ref, load_sem.at[3]),
        pltpu.make_async_copy(scale_hbm, scale_ref, load_sem.at[4]),
        pltpu.make_async_copy(shift_hbm, shift_ref, load_sem.at[5]),
    ]
    for i in (3, 0, 4, 5, 1, 2):
        loads[i].start()

    barrier = pltpu.get_barrier_semaphore()
    for k in range(1, ranks):
        pl.semaphore_signal(
            barrier, inc=1, device_id={"rows": lax.rem(me + k, ranks)}, device_id_type=MESH
        )
    for k in range(1, particles):
        pl.semaphore_signal(
            barrier,
            inc=1,
            device_id={"particle": lax.rem(mine + k, particles)},
            device_id_type=MESH,
        )

    if wz.shape[0] > wconv_hbm.shape[0]:
        tail = wz.shape[0] - wconv_hbm.shape[0]
        wz[wconv_hbm.shape[0] :] = jnp.zeros((tail, chans), bf16)

    chan_r = lax.broadcasted_iota(jnp.int32, (chans, LANES), 0)
    group_r = lax.broadcasted_iota(jnp.int32, (chans, LANES), 1) * per_group
    inside = (chan_r >= group_r) & (chan_r < group_r + per_group)
    to_group = jnp.where(inside, 1.0, 0.0).astype(f32)
    group_c = lax.broadcasted_iota(jnp.int32, (LANES, chans), 0) * per_group
    chan_c = lax.broadcasted_iota(jnp.int32, (LANES, chans), 1)
    inside = (chan_c >= group_c) & (chan_c < group_c + per_group)
    to_chan = jnp.where(inside, 1.0, 0.0).astype(f32)

    loads[3].wait()
    x32 = x_ref[...].astype(f32)
    sums = jnp.concatenate(
        [
            jnp.sum(x32, axis=0, keepdims=True),
            jnp.sum(x32 * x32, axis=0, keepdims=True),
            jnp.zeros((6, chans), f32),
        ],
        axis=0,
    )
    stat_own[...] = jnp.dot(sums, to_group, precision=HIGH, preferred_element_type=f32)
    stats[me] = stat_own[...]

    with jax.named_scope("barrier"):
        pl.semaphore_wait(barrier, ranks + particles - 2)

    def remote(src, dst, send, recv, where):
        return pltpu.make_async_remote_copy(
            src_ref=src,
            dst_ref=dst,
            send_sem=send,
            recv_sem=recv,
            device_id=where,
            device_id_type=MESH,
        )

    class Gather:
        def __init__(self, src, buf, rows, cuts, sent, near, far):
            self.src, self.buf, self.rows, self.cuts = src, buf, rows, cuts
            self.sent, self.near, self.far = sent, near, far
            self.pieces = range(len(cuts))

        def rows_of(self, slot, start, size):
            return self.buf.at[pl.ds(pl.multiple_of(slot * self.rows + start, GRAIN), size)]

        def send(self, slot, i, side, recv, own=False):
            start, size = self.cuts[i]
            dst = self.rows_of(slot, start, size)
            src = self.src.at[pl.ds(start, size)] if own else dst
            row = (a + side) * INNER + b if side else other
            return remote(src, dst, self.sent.at[side + 1], recv, {"rows": row})

        def along(self, origin, i, side, own=False):
            return self.send(origin * INNER + b, i, side, self.near.at[origin, i], own)

        def across(self, origin, i, own=False):
            return self.send(origin * INNER + b, i, 0, self.far.at[origin], own)

        def begin(self, pieces):
            for i in pieces:
                self.across(a, i, True).start()
                for side, onward in ((1, a + 1 < outer), (-1, a > 0)):

                    @pl.when(onward)
                    def _():
                        self.along(a, i, side, True).start()

        def keep(self):
            self.buf[pl.ds(pl.multiple_of(me * self.rows, GRAIN), self.rows)] = self.src[...]

        def sides(self, t):
            return ((a >= t, a - t, 1, a + 1 < outer), (a + t < outer, a + t, -1, a > 0))

        def order(self, t):
            return list(self.pieces)

        def step(self, t, pieces=None):
            for i in self.pieces if pieces is None else pieces:
                for present, origin, side, onward in self.sides(t):

                    @pl.when(present)
                    def _():
                        self.along(origin, i, 1).wait_recv()

                        @pl.when(onward)
                        def _():
                            self.along(origin, i, side).start()

                        self.across(origin, i).start()

        def far_slab(self, origin):
            slab = self.rows_of(origin * INNER + (1 - b), 0, self.rows)
            remote(slab, slab, self.sent.at[1], self.far.at[origin], {"rows": other}).wait_recv()

        def rest(self, t):
            if t == 0:
                self.far_slab(a)
                return
            for present, origin, _, _ in self.sides(t):

                @pl.when(present)
                def _():
                    self.far_slab(origin)

        def sent_all(self, side, rows):
            part = self.buf.at[0:rows]
            remote(part, part, self.sent.at[side + 1], self.far.at[0], {"rows": other}).wait_send()

        def finish(self):
            for v in range(outer):

                @pl.when(a == v)
                def _():
                    self.sent_all(0, outer * self.rows)
                    if v + 1 < outer:
                        self.sent_all(1, (v + 1) * self.rows)
                    if v > 0:
                        self.sent_all(-1, (outer - v) * self.rows)

    def each_of(t, column, fn):
        if t == 0:
            fn(a * INNER + column)
            return
        for present, origin in ((a >= t, a - t), (a + t < outer, a + t)):

            @pl.when(present)
            def _():
                fn(origin * INNER + column)

    def each_near(t, fn):
        each_of(t, b, fn)

    def each_far(t, fn):
        each_of(t, 1 - b, fn)

    def each_slot(t, fn):
        if t == 0:
            fn(me)
            fn(other)
            return
        for present, origin in ((a >= t, a - t), (a + t < outer, a + t)):

            @pl.when(present)
            def _():
                fn(origin * INNER + b)
                fn(origin * INNER + (1 - b))

    near_half = outer // 2
    first = Gather(x_ref, lat, tokens, cut_rows(tokens, CUT1), sent1, near1, far1)
    second = Gather(chunk, rt, csp, cut_rows(csp, CUT2), sent2, near2, far2)

    def stat_copy(k):
        return remote(
            stat_own, stats.at[me], ss.at[0], ss.at[1], {"rows": lax.rem(me + k, ranks)}
        )

    def stat_all():
        part = stats.at[0 : ranks - 1]
        return remote(part, part, ss.at[0], ss.at[1], {"rows": other})

    def w_copy(k):
        dest = lax.rem(me + k, ranks)
        return remote(wt.at[dest], wbuf.at[me], ws.at[0], wr.at[me], {"rows": dest})

    def w_slot(k):
        return lax.rem(me + ranks - k, ranks)

    def w_pass_on(k, j, where):
        slot = w_slot(k)
        return remote(wbuf.at[slot], wbuf.at[slot], ws.at[j], wr.at[slot], where)

    def w_arrived(k):
        w_pass_on(k, 1, {"rows": other}).wait_recv()

    def w_to_core(k):
        return w_pass_on(k, 1, {"particle": grp * CORES + (1 - core)})

    def w_to_group(k, g):
        return w_pass_on(k, 1 + g, {"particle": lax.rem(grp + g, groups) * CORES + core})

    with jax.named_scope("start"):
        for k in range(1, ranks):
            stat_copy(k).start()
        first.begin(first.pieces)

    with jax.named_scope("turn"):
        loads[0].wait()
        turned = wz[...].T
        for d in range(ranks):
            wt[d, 0:cs] = turned[d * cs : (d + 1) * cs]
            if csp != cs:
                wt[d, cs:csp] = jnp.zeros((csp - cs, wt.shape[2]), bf16)

    with jax.named_scope("start2"):
        for k in range(particles, ranks):

            @pl.when(mine == k % particles)
            def _():
                w_copy(k).start()

        for k in range(1, particles):

            @pl.when(mine == k % particles)
            def _():
                w_copy(k).start()

        first.keep()
        wbuf[me] = wt[me]

    def w_forward(k):
        q = k % particles

        @pl.when(mine == q)
        def _():
            w_arrived(k)
            for g in range(1, groups):
                w_to_group(k, g).start()
            w_to_core(k).start()

    def w_relay(k):
        q = k % particles

        @pl.when((core == q % CORES) & (grp != q // CORES))
        def _():
            w_arrived(k)
            w_to_core(k).start()

    def w_last(k):
        q = k % particles

        @pl.when(core != q % CORES)
        def _():
            w_arrived(k)

    low_end = a < near_half
    with jax.named_scope("kvw"):
        loads[1].wait()
        if cpad != chans:
            wqkv[...] = jnp.zeros_like(wqkv)
            for d in range(ranks):
                wqkv[d * csp : d * csp + cs] = wpad[d * cs : (d + 1) * cs]
        late = INNER * csp
        near_size = cpad // 2
        parts = (
            (jnp.where(low_end, 0, near_size), near_size, wnear),
            (jnp.where(low_end, near_size, late), near_size - late, wmid),
            (jnp.where(low_end, cpad - late, 0), late, wlate),
        )
        parts = [(pl.multiple_of(at, GRAIN), size, dst) for at, size, dst in parts]
        for at, size, dst in parts:
            for n in range(2 * tiles):
                dst[n * LANES : (n + 1) * LANES] = wqkv[
                    pl.ds(at, size), chans + n * LANES : chans + (n + 1) * LANES
                ].T
    with jax.named_scope("g1a"):
        for t in range(1, near_half):
            first.step(t)
    with jax.named_scope("stats"):
        stat_all().wait_recv()
        by_group = jnp.sum(stats[...], axis=0) / count
        mean_g = by_group[0:1]
        inverse = lax.rsqrt(by_group[1:2] - mean_g * mean_g + 1e-05)
        back = jnp.concatenate([mean_g, inverse, jnp.zeros((6, LANES), f32)], axis=0)
        spread = jnp.dot(back, to_chan, precision=HIGH, preferred_element_type=f32)
        mean_c, inverse_c = spread[0:1], spread[1:2]
        loads[4].wait()
        loads[5].wait()
        gain = 1.0 + scale_ref[...].reshape(1, chans)
        bias = shift_ref[...].reshape(1, chans)

    def activate(slot):
        at = pl.ds(pl.multiple_of(slot * tokens, GRAIN), tokens)
        v = lat[at].astype(f32)
        v = (v - mean_c) * inverse_c * gain + bias
        act[at] = (v / (1.0 + jnp.exp(-v))).astype(bf16)

    half = total // 2
    mine_half = lax.div(a, near_half)

    def conv(which):
        at = pl.multiple_of(which * half, LANES)
        yt[:, pl.ds(at, half)] = lax.dot_general(
            wd[...], act[pl.ds(at, half)], NT, preferred_element_type=f32
        )

    with jax.named_scope("wf2"):
        for k in range(particles, ranks):
            w_forward(k)
    with jax.named_scope("own"):
        activate(me)
    with jax.named_scope("g1b0"):
        for t in range(near_half, outer - 1):
            first.step(t, first.order(t)[:1])
    with jax.named_scope("wf1"):
        for k in range(1, min(particles, ranks)):
            w_forward(k)
    with jax.named_scope("g1b1"):
        for t in range(near_half, outer - 1):
            first.step(t, first.order(t)[1:])
    with jax.named_scope("act1"):
        first.rest(0)
        activate(other)
        for t in range(1, near_half):
            first.rest(t)
            each_slot(t, activate)
    with jax.named_scope("g1c"):
        first.step(outer - 1)
    with jax.named_scope("w2"):
        for k in range(1, ranks):
            w_relay(k)
    with jax.named_scope("act2"):
        for t in range(near_half, outer - 1):
            first.rest(t)
            each_slot(t, activate)
    with jax.named_scope("w3"):
        for k in range(1, ranks):
            w_last(k)
    with jax.named_scope("wd"):
        line = jnp.concatenate([wbuf[r][:, :share] for r in range(ranks)], axis=1)
        for tap in range(TAPS):
            wd[tap * csp : (tap + 1) * csp] = line[:, tap * chans : (tap + 1) * chans]
    with jax.named_scope("conv1"):
        conv(mine_half)
    with jax.named_scope("act3"):
        first.rest(outer - 1)
        each_slot(outer - 1, activate)
    with jax.named_scope("conv2"):
        pick = lax.broadcasted_iota(jnp.int32, (csp, chans), 0)
        at = lax.broadcasted_iota(jnp.int32, (csp, chans), 1)
        pick = jnp.where((at == me * cs + pick) & (pick < cs), 1.0, 0.0).astype(bf16)
        field[...] = lax.dot_general(pick, lat[...], NT, preferred_element_type=f32)
        conv(1 - mine_half)

    with jax.named_scope("taps"):
        lane = lax.broadcasted_iota(jnp.int32, (1, total), 1)
        column = lax.rem(lane, width)
        has_left = column > 0
        has_right = column < width - 1
        has_above = lane >= width
        has_below = lane < total - width

        def add_taps(i, carry):
            def tap(row, col):
                base = (row * 3 + col) * csp
                return yt[pl.ds(pl.multiple_of(base + i * GRAIN, GRAIN), GRAIN), :]

            cols = []
            for col in range(3):
                above = jnp.where(has_above, pltpu.roll(tap(0, col), width, 1), 0.0)
                below = jnp.where(has_below, pltpu.roll(tap(2, col), total - width, 1), 0.0)
                cols.append(tap(1, col) + above + below)
            left = jnp.where(has_left, pltpu.roll(cols[0], 1, 1), 0.0)
            right = jnp.where(has_right, pltpu.roll(cols[2], total - 1, 1), 0.0)
            at = pl.ds(pl.multiple_of(i * GRAIN, GRAIN), GRAIN)
            chunk[at] = (field[at] + (cols[1] + left + right)).astype(bf16)
            return carry

        for i in second.pieces:
            start, size = second.cuts[i]
            lax.fori_loop(start // GRAIN, (start + size) // GRAIN, add_taps, 0)
            second.begin([i])
        second.keep()

    own_r = lax.broadcasted_iota(jnp.int32, (csp, csp), 0)
    own_c = lax.broadcasted_iota(jnp.int32, (csp, csp), 1)
    same = (lax.div(own_r, per_group) == lax.div(own_c, per_group)) & (own_r < cs) & (own_c < cs)
    same = jnp.where(same, 1.0, 0.0).astype(f32)
    lane = lax.broadcasted_iota(jnp.int32, (csp, LANES), 1)

    def norm_copy(k):
        return remote(
            norm_own, norms.at[me], ns.at[0], nr.at[me], {"rows": lax.rem(me + k, ranks)}
        )

    with jax.named_scope("own"):
        v = chunk[...].astype(f32)
        both = jnp.where(
            lane == 0,
            jnp.sum(v, axis=1, keepdims=True),
            jnp.where(lane == 1, jnp.sum(v * v, axis=1, keepdims=True), 0.0),
        )
        both = jnp.dot(same, both, precision=HIGH, preferred_element_type=f32) / count
        mean = both[:, 0:1]
        inv = lax.rsqrt(both[:, 1:2] - mean * mean + 1e-05)
        both = jnp.where(lane == 0, mean, jnp.where(lane == 1, inv, 0.0))
        both = jnp.concatenate([both, jnp.zeros((LANES - csp, LANES), f32)], axis=0)
        norm_own[...] = both.T[0:8]
        for k in range(1, ranks):
            norm_copy(k).start()
        nt[pl.ds(pl.multiple_of(me * csp, GRAIN), csp)] = ((v - mean) * inv).astype(bf16)

    def normalize(slot):
        at = pl.ds(pl.multiple_of(slot * csp, GRAIN), csp)
        remote(norm_own, norms.at[slot], ns.at[0], nr.at[slot], {"rows": other}).wait_recv()
        both = norms[slot].T
        v = rt[at].astype(f32)
        nt[at] = ((v - both[:csp, 0:1]) * both[:csp, 1:2]).astype(bf16)

    step = 2 * LANES
    kv_rows = [slice(n * step, (n + 1) * step) for n in range(2 * chans // step)]

    def kv_part(i, rows):
        at, size, weights = parts[i]
        return jnp.dot(weights[rows], nt[pl.ds(at, size)], preferred_element_type=f32)

    with jax.named_scope("g2"):
        for t in range(1, outer):
            second.step(t)
            second.rest(t - 1)
            each_far(t - 1, normalize)
            each_near(t, normalize)
            if early and t == near_half:
                for rows in kv_rows:
                    kacc[rows] = kv_part(0, rows)

    with jax.named_scope("kv1"):
        row = lax.broadcasted_iota(jnp.int32, (tokens, total), 0)
        at = lax.broadcasted_iota(jnp.int32, (tokens, total), 1)
        pick = jnp.where(at == me * tokens + row, 1.0, 0.0).astype(bf16)

        def query_part(i):
            at, size, _ = parts[i]
            at = pl.ds(at, size)
            own = lax.dot_general(pick, nt[at], NT, preferred_element_type=f32).astype(bf16)
            return jnp.dot(own, wqkv[at, :chans], preferred_element_type=f32)

        query = query_part(0) + query_part(1)
        if early:
            for rows in kv_rows:
                kacc[rows] += kv_part(1, rows)
    with jax.named_scope("g2b"):
        second.rest(outer - 1)
        each_far(outer - 1, normalize)

    with jax.named_scope("qkv"):
        query = (query + query_part(2)).astype(bf16)
        for rows in kv_rows:
            head = kacc[rows] if early else kv_part(0, rows) + kv_part(1, rows)
            kvt[rows] = (head + kv_part(2, rows)).astype(bf16)
        resid = lax.dot_general(pick, rt[...], NT, preferred_element_type=f32)
        if cpad != chans:
            resid = jnp.concatenate(
                [resid[:, d * csp : d * csp + cs] for d in range(ranks)], axis=1
            )

    with jax.named_scope("attn"):
        pair = 2 * head_dim
        lane = lax.broadcasted_iota(jnp.int32, (tokens, pair), 1)
        low = lane < head_dim
        zero = jnp.zeros((tokens, pair), bf16)
        for h in range(HEADS // 2):
            q = query[:, h * pair : (h + 1) * pair]
            q = jnp.concatenate([jnp.where(low, q, zero), jnp.where(low, zero, q)], axis=0)
            scores = jnp.dot(
                q, kvt[h * pair : (h + 1) * pair], preferred_element_type=f32
            ) * (head_dim ** (-0.5))
            top = jnp.max(scores, axis=1, keepdims=True)
            weights = jnp.exp(scores - top)
            norm = jnp.sum(weights, axis=1, keepdims=True)
            mixed = (
                lax.dot_general(
                    weights.astype(bf16),
                    kvt[chans + h * pair : chans + (h + 1) * pair],
                    NT,
                    preferred_element_type=f32,
                )
                / norm
            )
            att[:, h * pair : (h + 1) * pair] = jnp.where(
                low, mixed[:tokens], mixed[tokens:]
            ).astype(bf16)
    def to_core(p, j):
        where = {"particle": grp * CORES + (1 - core)}
        return remote(blocks.at[p * tiles + j], blocks.at[p * tiles + j], ps.at[0], pr.at[0], where)

    def to_group(j, g, cross=0):
        there = 1 - core if cross else core
        where = {"particle": lax.rem(grp + g, groups) * CORES + there}
        recv = pr.at[1] if cross else pr.at[2 + (g - 1) * tiles + j]
        return remote(blocks.at[mine * tiles + j], blocks.at[mine * tiles + j], ps.at[groups if cross else g], recv, where)

    def from_group(j, g):
        part = blocks.at[of_group(g, core) * tiles + j]
        remote(part, part, ps.at[g], pr.at[2 + (g - 1) * tiles + j], {"rows": other}).wait_recv()

    def tiles_of(n, sem, recv=0):
        part = blocks.at[0:n]
        return remote(part, part, ps.at[sem], pr.at[recv], {"rows": other})

    passed = max(0, tiles - STRAIGHT)
    by_core = tiles + (groups - 1) * passed
    crossing = (groups - 1) * (tiles - passed)

    def of_group(g, side):
        return lax.rem(grp + groups - g, groups) * CORES + side

    with jax.named_scope("proj"):
        loads[2].wait()
        for j in range(tiles):
            if j % WIDE == 0:
                at = slice(j * LANES, min(j + WIDE, tiles) * LANES)
                wide = resid[:, at] + jnp.dot(
                    att[...], wout[:, at], preferred_element_type=f32
                )
            at = j % WIDE * LANES
            blocks[mine * tiles + j] = wide[:, at : at + LANES].astype(bf16)
            for g in range(1, groups):
                to_group(j, g).start()
            to_core(mine, j).start()
        for j in range(passed, tiles):
            for g in range(1, groups):
                to_group(j, g, 1).start()

    with jax.named_scope("resample"):
        for j in range(tiles):
            for g in range(1, groups):
                from_group(j, g)
                if j < passed:
                    to_core(of_group(g, core), j).start()
        tiles_of(by_core, 0).wait_recv()
        if crossing:
            tiles_of(crossing, 0, 1).wait_recv()
        for j in range(tiles):
            out_ref[:, j * LANES : (j + 1) * LANES] = blocks[anc_ref[mine] * tiles + j]
    with jax.named_scope("drain"):
        tiles_of(by_core, 0).wait_send()
        for g in range(1, groups):
            tiles_of(tiles, g).wait_send()
        if crossing:
            tiles_of(crossing, groups).wait_send()
        first.finish()
        second.finish()
        stat_all().wait_send()
        part = norms.at[0 : ranks - 1]
        remote(part, part, ns.at[0], nr.at[0], {"rows": other}).wait_send()
        for q in range(particles):
            count = len(range(q, ranks, particles)) - (q == 0)

            @pl.when(mine == q)
            def _():
                part = wbuf.at[0:count]
                for g in [0] + list(range(2, groups + 1)):
                    remote(part, part, ws.at[g], wr.at[0], {"rows": other}).wait_send()

        for c in range(CORES):
            count = sum(k % particles % CORES == c for k in range(1, ranks))

            @pl.when(core == c)
            def _():
                part = wbuf.at[0:count]
                remote(part, part, ws.at[1], wr.at[0], {"rows": other}).wait_send()


def per_device(latent, ada_scale, ada_shift, conv_weight, qkv_weight, out_weight, ancestors):
    _, rows_here, width, chans = latent.shape
    tokens = rows_here * width
    ranks = lax.axis_size("rows")
    particles = lax.axis_size("particle")
    groups = particles // CORES
    total = tokens * ranks
    share = conv_weight.shape[0]
    span = -(-share // LANES) * LANES
    if share % GRAIN:
        conv_weight = jnp.pad(conv_weight, ((0, span - share), (0, 0)))
    cs = chans // ranks
    csp = -(-cs // GRAIN) * GRAIN
    cpad = csp * ranks
    outer = ranks // INNER
    n1, n2 = len(cut_rows(tokens, CUT1)), len(cut_rows(csp, CUT2))
    early = outer <= 4
    dims = (rows_here, width, chans, ranks, particles, share, early)
    bf16, f32 = jnp.bfloat16, jnp.float32
    dma = pltpu.SemaphoreType.DMA
    out = pl.pallas_call(
        functools.partial(kernel, dims),
        out_shape=pltpu.VMEM((tokens, chans), bf16),
        in_specs=[pl.BlockSpec(memory_space=pltpu.SMEM)]
        + [pl.BlockSpec(memory_space=pl.ANY)] * 6,
        out_specs=pl.BlockSpec(memory_space=pltpu.VMEM),
        scratch_shapes=[
            pltpu.VMEM((tokens, chans), bf16),
            pltpu.VMEM(ada_scale.shape, f32),
            pltpu.VMEM(ada_shift.shape, f32),
            pltpu.VMEM((span, chans), bf16),
            pltpu.VMEM((ranks, csp, span), bf16),
            pltpu.VMEM((ranks, csp, span), bf16),
            pltpu.VMEM((TAPS * csp, chans), bf16),
            pltpu.VMEM((cpad, 3 * chans), bf16),
            pltpu.VMEM((GRAIN, LANES) if cpad == chans else qkv_weight.shape, bf16),
            pltpu.VMEM((2 * chans, cpad // 2), bf16),
            pltpu.VMEM((2 * chans, cpad // 2 - INNER * csp), bf16),
            pltpu.VMEM((2 * chans, INNER * csp), bf16),
            pltpu.VMEM((2 * chans, total) if early else (8, LANES), f32),
            pltpu.VMEM(out_weight.shape, bf16),
            pltpu.VMEM((total, chans), bf16),
            pltpu.VMEM((total, chans), bf16),
            pltpu.VMEM((TAPS * csp, total), f32),
            pltpu.VMEM((csp, total), f32),
            pltpu.VMEM((csp, total), bf16),
            pltpu.VMEM((cpad, total), bf16),
            pltpu.VMEM((cpad, total), bf16),
            pltpu.VMEM((2 * chans, total), bf16),
            pltpu.VMEM((tokens, chans), bf16),
            pltpu.VMEM((particles * (chans // LANES), tokens, LANES), bf16),
            pltpu.VMEM((8, LANES), f32),
            pltpu.VMEM((ranks, 8, LANES), f32),
            pltpu.VMEM((8, LANES), f32),
            pltpu.VMEM((ranks, 8, LANES), f32),
            dma((6,)),
            dma((1,)),
            dma((ranks,)),
            dma((1 + groups,)),
            dma((ranks,)),
            dma((2,)),
            dma((3,)),
            dma((outer, n1)),
            dma((outer,)),
            dma((3,)),
            dma((outer, n2)),
            dma((outer,)),
            dma((groups + 1,)),
            dma((2 + (groups - 1) * (chans // LANES),)),
        ],
        compiler_params=pltpu.CompilerParams(
            collective_id=0, has_side_effects=True, vmem_limit_bytes=64000 * 1024
        ),
        name="block",
    )(
        ancestors,
        latent.reshape(tokens, chans),
        ada_scale,
        ada_shift,
        conv_weight,
        qkv_weight,
        out_weight,
    )
    return out.reshape(latent.shape)


def solution(mesh):
    in_specs = (P("particle", "rows", None, None), P(), P(), P("rows", None), P(), P(), P())
    out_specs = P("particle", "rows", None, None)
    return jax.shard_map(
        per_device, mesh=mesh, in_specs=in_specs, out_specs=out_specs, check_vma=False
    )
```

```python
import functools
import math

import jax
import jax.numpy as jnp
from jax import lax
from jax.experimental import pallas as pl
from jax.experimental.pallas import tpu as pltpu
from jax.sharding import PartitionSpec as P

HEADS = 10
GROUPS = 32
INNER = 2
CUT1 = 2
CUT2 = 1
STRAIGHT = 2
WIDE = 2
DIRECT2 = 0
CORES = 2
LANES = 128
GRAIN = 16
TAPS = 9
MESH = pl.DeviceIdType.MESH
NT = (((1,), (1,)), ((), ()))
HIGH = lax.Precision.HIGHEST


def cut_rows(rows, grains):
    step = grains * GRAIN
    return [(at, min(step, rows - at)) for at in range(0, rows, step)]


def kernel(
    dims,
    anc_ref,
    x_hbm,
    scale_hbm,
    shift_hbm,
    wconv_hbm,
    wqkv_hbm,
    wout_hbm,
    out_ref,
    x_ref,
    scale_ref,
    shift_ref,
    wz,
    wt,
    wbuf,
    wd,
    wqkv,
    wpad,
    wnear,
    wmid,
    wlate,
    kacc,
    wout,
    lat,
    act,
    yt,
    field,
    chunk,
    rt,
    nt,
    kvt,
    att,
    own_rows,
    blocks,
    stat_own,
    stats,
    norm_own,
    norms,
    load_sem,
    ns,
    nr,
    ws,
    wr,
    ss,
    sent1,
    near1,
    far1,
    sent2,
    near2,
    far2,
    ps,
    pr,
):
    rows_here, width, chans, ranks, particles, share, early = dims
    tokens = rows_here * width
    total = tokens * ranks
    outer = ranks // INNER
    groups = particles // CORES
    cs = chans // ranks
    csp = chunk.shape[0]
    cpad = ranks * csp
    per_group = chans // GROUPS
    count = total * per_group
    head_dim = chans // HEADS
    tiles = chans // LANES
    fold = math.log2(head_dim) % 2 == 0
    bf16, f32 = jnp.bfloat16, jnp.float32
    me = lax.axis_index("rows")
    mine = lax.axis_index("particle")
    a = lax.div(me, INNER)
    b = lax.rem(me, INNER)
    other = a * INNER + (1 - b)
    grp = lax.div(mine, CORES)
    core = lax.rem(mine, CORES)

    conv_in = wz.at[0 : wconv_hbm.shape[0]]
    qkv_in = wqkv if cpad == chans else wpad
    loads = [
        pltpu.make_async_copy(wconv_hbm, conv_in, load_sem.at[0]),
        pltpu.make_async_copy(wqkv_hbm, qkv_in, load_sem.at[1]),
        pltpu.make_async_copy(wout_hbm, wout, load_sem.at[2]),
        pltpu.make_async_copy(x_hbm, x_ref, load_sem.at[3]),
        pltpu.make_async_copy(scale_hbm, scale_ref, load_sem.at[4]),
        pltpu.make_async_copy(shift_hbm, shift_ref, load_sem.at[5]),
    ]
    for i in (3, 0, 4, 5, 1, 2):
        loads[i].start()

    barrier = pltpu.get_barrier_semaphore()
    for k in range(1, ranks):
        pl.semaphore_signal(
            barrier, inc=1, device_id={"rows": lax.rem(me + k, ranks)}, device_id_type=MESH
        )
    for k in range(1, particles):
        pl.semaphore_signal(
            barrier,
            inc=1,
            device_id={"particle": lax.rem(mine + k, particles)},
            device_id_type=MESH,
        )

    if wz.shape[0] > wconv_hbm.shape[0]:
        tail = wz.shape[0] - wconv_hbm.shape[0]
        wz[wconv_hbm.shape[0] :] = jnp.zeros((tail, chans), bf16)

    chan_r = lax.broadcasted_iota(jnp.int32, (chans, LANES), 0)
    group_r = lax.broadcasted_iota(jnp.int32, (chans, LANES), 1) * per_group
    inside = (chan_r >= group_r) & (chan_r < group_r + per_group)
    to_group = jnp.where(inside, 1.0, 0.0).astype(f32)
    group_c = lax.broadcasted_iota(jnp.int32, (LANES, chans), 0) * per_group
    chan_c = lax.broadcasted_iota(jnp.int32, (LANES, chans), 1)
    inside = (chan_c >= group_c) & (chan_c < group_c + per_group)
    to_chan = jnp.where(inside, 1.0, 0.0).astype(f32)

    loads[3].wait()
    x32 = x_ref[...].astype(f32)
    sums = jnp.concatenate(
        [
            jnp.sum(x32, axis=0, keepdims=True),
            jnp.sum(x32 * x32, axis=0, keepdims=True),
            jnp.zeros((6, chans), f32),
        ],
        axis=0,
    )
    stat_own[...] = jnp.dot(sums, to_group, precision=HIGH, preferred_element_type=f32)
    stats[me] = stat_own[...]

    with jax.named_scope("barrier"):
        pl.semaphore_wait(barrier, ranks + particles - 2)

    def remote(src, dst, send, recv, where):
        return pltpu.make_async_remote_copy(
            src_ref=src,
            dst_ref=dst,
            send_sem=send,
            recv_sem=recv,
            device_id=where,
            device_id_type=MESH,
        )

    class Gather:
        def __init__(self, src, buf, rows, cuts, sent, near, far):
            self.src, self.buf, self.rows, self.cuts = src, buf, rows, cuts
            self.sent, self.near, self.far = sent, near, far
            self.pieces = range(len(cuts))

        def rows_of(self, slot, start, size):
            return self.buf.at[pl.ds(pl.multiple_of(slot * self.rows + start, GRAIN), size)]

        def send(self, slot, i, side, recv, own=False):
            start, size = self.cuts[i]
            dst = self.rows_of(slot, start, size)
            src = self.src.at[pl.ds(start, size)] if own else dst
            row = (a + side) * INNER + b if side else other
            return remote(src, dst, self.sent.at[side + 1], recv, {"rows": row})

        def along(self, origin, i, side, own=False):
            return self.send(origin * INNER + b, i, side, self.near.at[origin, i], own)

        def across(self, origin, i, own=False):
            return self.send(origin * INNER + b, i, 0, self.far.at[origin], own)

        def begin(self, pieces):
            for i in pieces:
                self.across(a, i, True).start()
                for side, onward in ((1, a + 1 < outer), (-1, a > 0)):

                    @pl.when(onward)
                    def _():
                        self.along(a, i, side, True).start()

        def keep(self):
            self.buf[pl.ds(pl.multiple_of(me * self.rows, GRAIN), self.rows)] = self.src[...]

        def sides(self, t):
            return ((a >= t, a - t, 1, a + 1 < outer), (a + t < outer, a + t, -1, a > 0))

        def order(self, t):
            return list(self.pieces)

        def step(self, t, pieces=None):
            for i in self.pieces if pieces is None else pieces:
                for present, origin, side, onward in self.sides(t):

                    @pl.when(present)
                    def _():
                        self.along(origin, i, 1).wait_recv()

                        @pl.when(onward)
                        def _():
                            self.along(origin, i, side).start()

                        self.across(origin, i).start()

        def far_slab(self, origin):
            slab = self.rows_of(origin * INNER + (1 - b), 0, self.rows)
            remote(slab, slab, self.sent.at[1], self.far.at[origin], {"rows": other}).wait_recv()

        def rest(self, t):
            if t == 0:
                self.far_slab(a)
                return
            for present, origin, _, _ in self.sides(t):

                @pl.when(present)
                def _():
                    self.far_slab(origin)

        def sent_all(self, side, rows):
            part = self.buf.at[0:rows]
            remote(part, part, self.sent.at[side + 1], self.far.at[0], {"rows": other}).wait_send()

        def finish(self):
            for v in range(outer):

                @pl.when(a == v)
                def _():
                    self.sent_all(0, outer * self.rows)
                    if v + 1 < outer:
                        self.sent_all(1, (v + 1) * self.rows)
                    if v > 0:
                        self.sent_all(-1, (outer - v) * self.rows)

    def each_of(t, column, fn):
        if t == 0:
            fn(a * INNER + column)
            return
        for present, origin in ((a >= t, a - t), (a + t < outer, a + t)):

            @pl.when(present)
            def _():
                fn(origin * INNER + column)

    def each_near(t, fn):
        each_of(t, b, fn)

    def each_far(t, fn):
        each_of(t, 1 - b, fn)

    def each_slot(t, fn):
        if t == 0:
            fn(me)
            fn(other)
            return
        for present, origin in ((a >= t, a - t), (a + t < outer, a + t)):

            @pl.when(present)
            def _():
                fn(origin * INNER + b)
                fn(origin * INNER + (1 - b))

    near_half = outer // 2
    first = Gather(x_ref, lat, tokens, cut_rows(tokens, CUT1), sent1, near1, far1)
    second = Gather(chunk, rt, csp, cut_rows(csp, CUT2), sent2, near2, far2)

    def stat_copy(k):
        return remote(
            stat_own, stats.at[me], ss.at[0], ss.at[1], {"rows": lax.rem(me + k, ranks)}
        )

    def stat_all():
        part = stats.at[0 : ranks - 1]
        return remote(part, part, ss.at[0], ss.at[1], {"rows": other})

    def w_copy(k):
        dest = lax.rem(me + k, ranks)
        return remote(wt.at[dest], wbuf.at[me], ws.at[0], wr.at[me], {"rows": dest})

    def w_slot(k):
        return lax.rem(me + ranks - k, ranks)

    def w_pass_on(k, j, where):
        slot = w_slot(k)
        return remote(wbuf.at[slot], wbuf.at[slot], ws.at[j], wr.at[slot], where)

    def w_arrived(k):
        w_pass_on(k, 1, {"rows": other}).wait_recv()

    def w_to_core(k):
        return w_pass_on(k, 1, {"particle": grp * CORES + (1 - core)})

    def w_to_group(k, g):
        return w_pass_on(k, 1 + g, {"particle": lax.rem(grp + g, groups) * CORES + core})

    with jax.named_scope("start"):
        for k in range(1, ranks):
            stat_copy(k).start()
        first.begin(first.pieces)

    with jax.named_scope("turn"):
        loads[0].wait()
        turned = wz[...].T
        for d in range(ranks):
            wt[d, 0:cs] = turned[d * cs : (d + 1) * cs]
            if csp != cs:
                wt[d, cs:csp] = jnp.zeros((csp - cs, wt.shape[2]), bf16)

    with jax.named_scope("start2"):
        for k in range(1, particles):

            @pl.when(mine == k % particles)
            def _():
                w_copy(k).start()

        for k in range(particles, ranks):

            @pl.when(mine == k % particles)
            def _():
                w_copy(k).start()

        first.keep()
        wbuf[me] = wt[me]

    def w_forward(k):
        q = k % particles

        @pl.when(mine == q)
        def _():
            w_arrived(k)
            for g in range(1, groups):
                w_to_group(k, g).start()
            w_to_core(k).start()

    def w_relay(k):
        q = k % particles

        @pl.when((core == q % CORES) & (grp != q // CORES))
        def _():
            w_arrived(k)
            w_to_core(k).start()

    def w_last(k):
        q = k % particles

        @pl.when(core != q % CORES)
        def _():
            w_arrived(k)

    low_end = a < near_half
    with jax.named_scope("kvw"):
        loads[1].wait()
        if cpad != chans:
            wqkv[...] = jnp.zeros_like(wqkv)
            for d in range(ranks):
                wqkv[d * csp : d * csp + cs] = wpad[d * cs : (d + 1) * cs]
        late = INNER * csp
        near_size = cpad // 2
        parts = (
            (jnp.where(low_end, 0, near_size), near_size, wnear),
            (jnp.where(low_end, near_size, late), near_size - late, wmid),
            (jnp.where(low_end, cpad - late, 0), late, wlate),
        )
        parts = [(pl.multiple_of(at, GRAIN), size, dst) for at, size, dst in parts]
        for at, size, dst in parts:
            for n in range(2 * tiles):
                dst[n * LANES : (n + 1) * LANES] = wqkv[
                    pl.ds(at, size), chans + n * LANES : chans + (n + 1) * LANES
                ].T
    with jax.named_scope("g1a"):
        for t in range(1, near_half):
            first.step(t)
    with jax.named_scope("stats"):
        stat_all().wait_recv()
        by_group = jnp.sum(stats[...], axis=0) / count
        mean_g = by_group[0:1]
        inverse = lax.rsqrt(by_group[1:2] - mean_g * mean_g + 1e-05)
        back = jnp.concatenate([mean_g, inverse, jnp.zeros((6, LANES), f32)], axis=0)
        spread = jnp.dot(back, to_chan, precision=HIGH, preferred_element_type=f32)
        mean_c, inverse_c = spread[0:1], spread[1:2]
        loads[4].wait()
        loads[5].wait()
        gain = 1.0 + scale_ref[...].reshape(1, chans)
        bias = shift_ref[...].reshape(1, chans)

    def activate(slot):
        at = pl.ds(pl.multiple_of(slot * tokens, GRAIN), tokens)
        v = lat[at].astype(f32)
        v = (v - mean_c) * inverse_c * gain + bias
        act[at] = (v / (1.0 + jnp.exp(-v))).astype(bf16)

    half = total // 2
    mine_half = lax.div(a, near_half)

    def conv(which):
        at = pl.multiple_of(which * half, LANES)
        yt[:, pl.ds(at, half)] = lax.dot_general(
            wd[...], act[pl.ds(at, half)], NT, preferred_element_type=f32
        )

    with jax.named_scope("own"):
        activate(me)
    with jax.named_scope("wf1"):
        for k in range(1, min(particles, ranks)):
            w_forward(k)
    with jax.named_scope("g1b0"):
        for t in range(near_half, outer - 1):
            first.step(t, first.order(t)[:1])
    with jax.named_scope("wf2"):
        for k in range(particles, ranks):
            w_forward(k)
    with jax.named_scope("g1b1"):
        for t in range(near_half, outer - 1):
            first.step(t, first.order(t)[1:])
    with jax.named_scope("act1"):
        first.rest(0)
        activate(other)
        for t in range(1, near_half):
            first.rest(t)
            each_slot(t, activate)
    with jax.named_scope("g1c"):
        first.step(outer - 1)
    with jax.named_scope("w2"):
        for k in range(1, ranks):
            w_relay(k)
    with jax.named_scope("act2"):
        for t in range(near_half, outer - 1):
            first.rest(t)
            each_slot(t, activate)
    with jax.named_scope("w3"):
        for k in range(1, ranks):
            w_last(k)
    with jax.named_scope("wd"):
        line = jnp.concatenate([wbuf[r][:, :share] for r in range(ranks)], axis=1)
        for tap in range(TAPS):
            wd[tap * csp : (tap + 1) * csp] = line[:, tap * chans : (tap + 1) * chans]
    with jax.named_scope("conv1"):
        conv(mine_half)
    with jax.named_scope("act3"):
        first.rest(outer - 1)
        each_slot(outer - 1, activate)
    with jax.named_scope("conv2"):
        pick = lax.broadcasted_iota(jnp.int32, (csp, chans), 0)
        at = lax.broadcasted_iota(jnp.int32, (csp, chans), 1)
        pick = jnp.where((at == me * cs + pick) & (pick < cs), 1.0, 0.0).astype(bf16)
        field[...] = lax.dot_general(pick, lat[...], NT, preferred_element_type=f32)
        conv(1 - mine_half)

    with jax.named_scope("taps"):
        lane = lax.broadcasted_iota(jnp.int32, (1, total), 1)
        column = lax.rem(lane, width)
        has_left = column > 0
        has_right = column < width - 1
        has_above = lane >= width
        has_below = lane < total - width

        def add_taps(i, carry):
            def tap(row, col):
                base = (row * 3 + col) * csp
                return yt[pl.ds(pl.multiple_of(base + i * GRAIN, GRAIN), GRAIN), :]

            cols = []
            for col in range(3):
                above = jnp.where(has_above, pltpu.roll(tap(0, col), width, 1), 0.0)
                below = jnp.where(has_below, pltpu.roll(tap(2, col), total - width, 1), 0.0)
                cols.append(tap(1, col) + above + below)
            left = jnp.where(has_left, pltpu.roll(cols[0], 1, 1), 0.0)
            right = jnp.where(has_right, pltpu.roll(cols[2], total - 1, 1), 0.0)
            at = pl.ds(pl.multiple_of(i * GRAIN, GRAIN), GRAIN)
            chunk[at] = (field[at] + (cols[1] + left + right)).astype(bf16)
            return carry

        for i in second.pieces:
            start, size = second.cuts[i]
            lax.fori_loop(start // GRAIN, (start + size) // GRAIN, add_taps, 0)
            second.begin([i])
        second.keep()

    own_r = lax.broadcasted_iota(jnp.int32, (csp, csp), 0)
    own_c = lax.broadcasted_iota(jnp.int32, (csp, csp), 1)
    same = (lax.div(own_r, per_group) == lax.div(own_c, per_group)) & (own_r < cs) & (own_c < cs)
    same = jnp.where(same, 1.0, 0.0).astype(f32)
    lane = lax.broadcasted_iota(jnp.int32, (csp, LANES), 1)

    def norm_copy(k):
        return remote(
            norm_own, norms.at[me], ns.at[0], nr.at[me], {"rows": lax.rem(me + k, ranks)}
        )

    with jax.named_scope("own"):
        v = chunk[...].astype(f32)
        both = jnp.where(
            lane == 0,
            jnp.sum(v, axis=1, keepdims=True),
            jnp.where(lane == 1, jnp.sum(v * v, axis=1, keepdims=True), 0.0),
        )
        both = jnp.dot(same, both, precision=HIGH, preferred_element_type=f32) / count
        mean = both[:, 0:1]
        inv = lax.rsqrt(both[:, 1:2] - mean * mean + 1e-05)
        both = jnp.where(lane == 0, mean, jnp.where(lane == 1, inv, 0.0))
        both = jnp.concatenate([both, jnp.zeros((LANES - csp, LANES), f32)], axis=0)
        norm_own[...] = both.T[0:8]
        for k in range(1, ranks):
            norm_copy(k).start()
        nt[pl.ds(pl.multiple_of(me * csp, GRAIN), csp)] = ((v - mean) * inv).astype(bf16)

    def normalize(slot):
        at = pl.ds(pl.multiple_of(slot * csp, GRAIN), csp)
        remote(norm_own, norms.at[slot], ns.at[0], nr.at[slot], {"rows": other}).wait_recv()
        both = norms[slot].T
        v = rt[at].astype(f32)
        nt[at] = ((v - both[:csp, 0:1]) * both[:csp, 1:2]).astype(bf16)

    step = 2 * LANES
    kv_rows = [slice(n * step, (n + 1) * step) for n in range(2 * chans // step)]

    def kv_part(i, rows):
        at, size, weights = parts[i]
        return jnp.dot(weights[rows], nt[pl.ds(at, size)], preferred_element_type=f32)

    with jax.named_scope("g2"):
        for t in range(1, outer):
            second.step(t)
            second.rest(t - 1)
            each_far(t - 1, normalize)
            each_near(t, normalize)
            if early and t == near_half:
                for rows in kv_rows:
                    kacc[rows] = kv_part(0, rows)

    with jax.named_scope("kv1"):
        row = lax.broadcasted_iota(jnp.int32, (tokens, total), 0)
        at = lax.broadcasted_iota(jnp.int32, (tokens, total), 1)
        pick = jnp.where(at == me * tokens + row, 1.0, 0.0).astype(bf16)

        def query_part(i):
            at, size, _ = parts[i]
            at = pl.ds(at, size)
            own = lax.dot_general(pick, nt[at], NT, preferred_element_type=f32).astype(bf16)
            return jnp.dot(own, wqkv[at, :chans], preferred_element_type=f32)

        query = query_part(0) + query_part(1)
        if cpad == chans:
            ahead = pl.ds(pl.multiple_of(jnp.where(low_end, 0, late), GRAIN), cpad - late)
            own = lax.dot_general(pick, rt[ahead], NT, preferred_element_type=f32)

            @pl.when(low_end)
            def _():
                own_rows[:, : chans - late] = own

            @pl.when(jnp.logical_not(low_end))
            def _():
                own_rows[:, late:] = own

        if early:
            for rows in kv_rows:
                kacc[rows] += kv_part(1, rows)
    with jax.named_scope("g2b"):
        second.rest(outer - 1)
        each_far(outer - 1, normalize)

    with jax.named_scope("qkv"):
        query = (query + query_part(2)).astype(bf16)
        if fold:
            query = (query.astype(f32) * head_dim ** (-0.5)).astype(bf16)
        for rows in kv_rows:
            head = kacc[rows] if early else kv_part(0, rows) + kv_part(1, rows)
            kvt[rows] = (head + kv_part(2, rows)).astype(bf16)
        if cpad == chans:
            own = lax.dot_general(
                pick, rt[pl.ds(parts[2][0], late)], NT, preferred_element_type=f32
            )

            @pl.when(low_end)
            def _():
                own_rows[:, chans - late :] = own

            @pl.when(jnp.logical_not(low_end))
            def _():
                own_rows[:, :late] = own

        else:
            resid = lax.dot_general(pick, rt[...], NT, preferred_element_type=f32)
            own_rows[...] = jnp.concatenate(
                [resid[:, d * csp : d * csp + cs] for d in range(ranks)], axis=1
            )

    with jax.named_scope("attn"):
        pair = 2 * head_dim
        lane = lax.broadcasted_iota(jnp.int32, (tokens, pair), 1)
        low = lane < head_dim
        zero = jnp.zeros((tokens, pair), bf16)
        for h in range(HEADS // 2):
            q = query[:, h * pair : (h + 1) * pair]
            q = jnp.concatenate([jnp.where(low, q, zero), jnp.where(low, zero, q)], axis=0)
            scores = jnp.dot(
                q, kvt[h * pair : (h + 1) * pair], preferred_element_type=f32
            )
            if not fold:
                scores = scores * (head_dim ** (-0.5))
            top = jnp.max(scores, axis=1, keepdims=True)
            weights = jnp.exp(scores - top)
            norm = jnp.sum(weights, axis=1, keepdims=True)
            mixed = (
                lax.dot_general(
                    weights.astype(bf16),
                    kvt[chans + h * pair : chans + (h + 1) * pair],
                    NT,
                    preferred_element_type=f32,
                )
                / norm
            )
            att[:, h * pair : (h + 1) * pair] = jnp.where(
                low, mixed[:tokens], mixed[tokens:]
            ).astype(bf16)
    def to_core(p, j):
        where = {"particle": grp * CORES + (1 - core)}
        return remote(blocks.at[p * tiles + j], blocks.at[p * tiles + j], ps.at[0], pr.at[0], where)

    def to_group(j, g, cross=0):
        there = 1 - core if cross else core
        where = {"particle": lax.rem(grp + g, groups) * CORES + there}
        recv = pr.at[1] if cross else pr.at[2 + (g - 1) * tiles + j]
        return remote(blocks.at[mine * tiles + j], blocks.at[mine * tiles + j], ps.at[groups if cross else g], recv, where)

    def from_group(j, g):
        part = blocks.at[of_group(g, core) * tiles + j]
        remote(part, part, ps.at[g], pr.at[2 + (g - 1) * tiles + j], {"rows": other}).wait_recv()

    def tiles_of(n, sem, recv=0):
        part = blocks.at[0:n]
        return remote(part, part, ps.at[sem], pr.at[recv], {"rows": other})

    passed = max(0, tiles - STRAIGHT)
    by_core = tiles + (groups - 1) * passed
    crossing = (groups - 1) * (tiles - passed)

    def of_group(g, side):
        return lax.rem(grp + groups - g, groups) * CORES + side

    with jax.named_scope("proj"):
        loads[2].wait()
        for j in range(tiles):
            if j % WIDE == 0:
                at = slice(j * LANES, min(j + WIDE, tiles) * LANES)
                wide = own_rows[:, at] + jnp.dot(
                    att[...], wout[:, at], preferred_element_type=f32
                )
            at = j % WIDE * LANES
            blocks[mine * tiles + j] = wide[:, at : at + LANES].astype(bf16)
            for g in range(1, groups):
                to_group(j, g).start()
            to_core(mine, j).start()
        for j in range(passed, tiles):
            for g in range(1, groups):
                to_group(j, g, 1).start()

    with jax.named_scope("resample"):
        for j in range(tiles):
            for g in range(1, groups):
                from_group(j, g)
                if j < passed:
                    to_core(of_group(g, core), j).start()
        tiles_of(by_core, 0).wait_recv()
        if crossing:
            tiles_of(crossing, 0, 1).wait_recv()
        for j in range(tiles):
            out_ref[:, j * LANES : (j + 1) * LANES] = blocks[anc_ref[mine] * tiles + j]
    with jax.named_scope("drain"):
        tiles_of(by_core, 0).wait_send()
        for g in range(1, groups):
            tiles_of(tiles, g).wait_send()
        if crossing:
            tiles_of(crossing, groups).wait_send()
        first.finish()
        second.finish()
        stat_all().wait_send()
        part = norms.at[0 : ranks - 1]
        remote(part, part, ns.at[0], nr.at[0], {"rows": other}).wait_send()
        for q in range(particles):
            count = len(range(q, ranks, particles)) - (q == 0)

            @pl.when(mine == q)
            def _():
                part = wbuf.at[0:count]
                for g in [0] + list(range(2, groups + 1)):
                    remote(part, part, ws.at[g], wr.at[0], {"rows": other}).wait_send()

        for c in range(CORES):
            count = sum(k % particles % CORES == c for k in range(1, ranks))

            @pl.when(core == c)
            def _():
                part = wbuf.at[0:count]
                remote(part, part, ws.at[1], wr.at[0], {"rows": other}).wait_send()


def per_device(latent, ada_scale, ada_shift, conv_weight, qkv_weight, out_weight, ancestors):
    _, rows_here, width, chans = latent.shape
    tokens = rows_here * width
    ranks = lax.axis_size("rows")
    particles = lax.axis_size("particle")
    groups = particles // CORES
    total = tokens * ranks
    share = conv_weight.shape[0]
    span = -(-share // LANES) * LANES
    if share % GRAIN:
        conv_weight = jnp.pad(conv_weight, ((0, span - share), (0, 0)))
    cs = chans // ranks
    csp = -(-cs // GRAIN) * GRAIN
    cpad = csp * ranks
    outer = ranks // INNER
    n1, n2 = len(cut_rows(tokens, CUT1)), len(cut_rows(csp, CUT2))
    early = outer <= 4
    dims = (rows_here, width, chans, ranks, particles, share, early)
    bf16, f32 = jnp.bfloat16, jnp.float32
    dma = pltpu.SemaphoreType.DMA
    out = pl.pallas_call(
        functools.partial(kernel, dims),
        out_shape=pltpu.VMEM((tokens, chans), bf16),
        in_specs=[pl.BlockSpec(memory_space=pltpu.SMEM)]
        + [pl.BlockSpec(memory_space=pl.ANY)] * 6,
        out_specs=pl.BlockSpec(memory_space=pltpu.VMEM),
        scratch_shapes=[
            pltpu.VMEM((tokens, chans), bf16),
            pltpu.VMEM(ada_scale.shape, f32),
            pltpu.VMEM(ada_shift.shape, f32),
            pltpu.VMEM((span, chans), bf16),
            pltpu.VMEM((ranks, csp, span), bf16),
            pltpu.VMEM((ranks, csp, span), bf16),
            pltpu.VMEM((TAPS * csp, chans), bf16),
            pltpu.VMEM((cpad, 3 * chans), bf16),
            pltpu.VMEM((GRAIN, LANES) if cpad == chans else qkv_weight.shape, bf16),
            pltpu.VMEM((2 * chans, cpad // 2), bf16),
            pltpu.VMEM((2 * chans, cpad // 2 - INNER * csp), bf16),
            pltpu.VMEM((2 * chans, INNER * csp), bf16),
            pltpu.VMEM((2 * chans, total) if early else (8, LANES), f32),
            pltpu.VMEM(out_weight.shape, bf16),
            pltpu.VMEM((total, chans), bf16),
            pltpu.VMEM((total, chans), bf16),
            pltpu.VMEM((TAPS * csp, total), f32),
            pltpu.VMEM((csp, total), f32),
            pltpu.VMEM((csp, total), bf16),
            pltpu.VMEM((cpad, total), bf16),
            pltpu.VMEM((cpad, total), bf16),
            pltpu.VMEM((2 * chans, total), bf16),
            pltpu.VMEM((tokens, chans), bf16),
            pltpu.VMEM((tokens, chans), f32),
            pltpu.VMEM((particles * (chans // LANES), tokens, LANES), bf16),
            pltpu.VMEM((8, LANES), f32),
            pltpu.VMEM((ranks, 8, LANES), f32),
            pltpu.VMEM((8, LANES), f32),
            pltpu.VMEM((ranks, 8, LANES), f32),
            dma((6,)),
            dma((1,)),
            dma((ranks,)),
            dma((1 + groups,)),
            dma((ranks,)),
            dma((2,)),
            dma((3,)),
            dma((outer, n1)),
            dma((outer,)),
            dma((3,)),
            dma((outer, n2)),
            dma((outer,)),
            dma((groups + 1,)),
            dma((2 + (groups - 1) * (chans // LANES),)),
        ],
        compiler_params=pltpu.CompilerParams(
            collective_id=0, has_side_effects=True, vmem_limit_bytes=64000 * 1024
        ),
        name="block",
    )(
        ancestors,
        latent.reshape(tokens, chans),
        ada_scale,
        ada_shift,
        conv_weight,
        qkv_weight,
        out_weight,
    )
    return out.reshape(latent.shape)


def solution(mesh):
    in_specs = (P("particle", "rows", None, None), P(), P(), P("rows", None), P(), P(), P())
    out_specs = P("particle", "rows", None, None)
    return jax.shard_map(
        per_device, mesh=mesh, in_specs=in_specs, out_specs=out_specs, check_vma=False
    )
```

```python
import functools
import math

import jax
import jax.numpy as jnp
from jax import lax
from jax.experimental import pallas as pl
from jax.experimental.pallas import tpu as pltpu
from jax.sharding import PartitionSpec as P

HEADS = 10
GROUPS = 32
INNER = 2
CUT1 = 2
CUT2 = 1
STRAIGHT = 2
WIDE = 2
DIRECT2 = 0
CORES = 2
LANES = 128
GRAIN = 16
TAPS = 9
MESH = pl.DeviceIdType.MESH
NT = (((1,), (1,)), ((), ()))
HIGH = lax.Precision.HIGHEST


def cut_rows(rows, grains):
    step = grains * GRAIN
    return [(at, min(step, rows - at)) for at in range(0, rows, step)]


def kernel(
    dims,
    anc_ref,
    x_hbm,
    scale_hbm,
    shift_hbm,
    wconv_hbm,
    wqkv_hbm,
    wout_hbm,
    out_ref,
    x_ref,
    scale_ref,
    shift_ref,
    wz,
    wt,
    wbuf,
    wd,
    wqkv,
    wpad,
    wnear,
    wmid,
    wlate,
    kacc,
    wout,
    lat,
    act,
    yt,
    field,
    chunk,
    rt,
    nt,
    kvt,
    att,
    own_rows,
    blocks,
    stat_own,
    stats,
    norm_own,
    norms,
    load_sem,
    ns,
    nr,
    ws,
    wr,
    ss,
    sent1,
    near1,
    far1,
    sent2,
    near2,
    far2,
    ps,
    pr,
):
    rows_here, width, chans, ranks, particles, share, early = dims
    tokens = rows_here * width
    total = tokens * ranks
    outer = ranks // INNER
    groups = particles // CORES
    cs = chans // ranks
    csp = chunk.shape[0]
    cpad = ranks * csp
    per_group = chans // GROUPS
    count = total * per_group
    head_dim = chans // HEADS
    tiles = chans // LANES
    fold = math.log2(head_dim) % 2 == 0
    bf16, f32 = jnp.bfloat16, jnp.float32
    me = lax.axis_index("rows")
    mine = lax.axis_index("particle")
    a = lax.div(me, INNER)
    b = lax.rem(me, INNER)
    other = a * INNER + (1 - b)
    grp = lax.div(mine, CORES)
    core = lax.rem(mine, CORES)

    conv_in = wz.at[0 : wconv_hbm.shape[0]]
    qkv_in = wqkv if cpad == chans else wpad
    loads = [
        pltpu.make_async_copy(wconv_hbm, conv_in, load_sem.at[0]),
        pltpu.make_async_copy(wqkv_hbm, qkv_in, load_sem.at[1]),
        pltpu.make_async_copy(wout_hbm, wout, load_sem.at[2]),
        pltpu.make_async_copy(x_hbm, x_ref, load_sem.at[3]),
        pltpu.make_async_copy(scale_hbm, scale_ref, load_sem.at[4]),
        pltpu.make_async_copy(shift_hbm, shift_ref, load_sem.at[5]),
    ]
    for i in (3, 0, 4, 5, 1, 2):
        loads[i].start()

    barrier = pltpu.get_barrier_semaphore()
    for k in range(1, ranks):
        pl.semaphore_signal(
            barrier, inc=1, device_id={"rows": lax.rem(me + k, ranks)}, device_id_type=MESH
        )
    for k in range(1, particles):
        pl.semaphore_signal(
            barrier,
            inc=1,
            device_id={"particle": lax.rem(mine + k, particles)},
            device_id_type=MESH,
        )

    if wz.shape[0] > wconv_hbm.shape[0]:
        tail = wz.shape[0] - wconv_hbm.shape[0]
        wz[wconv_hbm.shape[0] :] = jnp.zeros((tail, chans), bf16)

    chan_r = lax.broadcasted_iota(jnp.int32, (chans, LANES), 0)
    group_r = lax.broadcasted_iota(jnp.int32, (chans, LANES), 1) * per_group
    inside = (chan_r >= group_r) & (chan_r < group_r + per_group)
    to_group = jnp.where(inside, 1.0, 0.0).astype(f32)
    group_c = lax.broadcasted_iota(jnp.int32, (LANES, chans), 0) * per_group
    chan_c = lax.broadcasted_iota(jnp.int32, (LANES, chans), 1)
    inside = (chan_c >= group_c) & (chan_c < group_c + per_group)
    to_chan = jnp.where(inside, 1.0, 0.0).astype(f32)

    with jax.named_scope("barrier"):
        pl.semaphore_wait(barrier, ranks + particles - 2)

    def remote(src, dst, send, recv, where):
        return pltpu.make_async_remote_copy(
            src_ref=src,
            dst_ref=dst,
            send_sem=send,
            recv_sem=recv,
            device_id=where,
            device_id_type=MESH,
        )

    class Gather:
        def __init__(self, src, buf, rows, cuts, sent, near, far):
            self.src, self.buf, self.rows, self.cuts = src, buf, rows, cuts
            self.sent, self.near, self.far = sent, near, far
            self.pieces = range(len(cuts))

        def rows_of(self, slot, start, size):
            return self.buf.at[pl.ds(pl.multiple_of(slot * self.rows + start, GRAIN), size)]

        def send(self, slot, i, side, recv, own=False):
            start, size = self.cuts[i]
            dst = self.rows_of(slot, start, size)
            src = self.src.at[pl.ds(start, size)] if own else dst
            row = (a + side) * INNER + b if side else other
            return remote(src, dst, self.sent.at[side + 1], recv, {"rows": row})

        def along(self, origin, i, side, own=False):
            return self.send(origin * INNER + b, i, side, self.near.at[origin, i], own)

        def across(self, origin, i, own=False):
            return self.send(origin * INNER + b, i, 0, self.far.at[origin], own)

        def begin(self, pieces):
            for i in pieces:
                self.across(a, i, True).start()
                for side, onward in ((1, a + 1 < outer), (-1, a > 0)):

                    @pl.when(onward)
                    def _():
                        self.along(a, i, side, True).start()

        def keep(self):
            self.buf[pl.ds(pl.multiple_of(me * self.rows, GRAIN), self.rows)] = self.src[...]

        def sides(self, t):
            return ((a >= t, a - t, 1, a + 1 < outer), (a + t < outer, a + t, -1, a > 0))

        def order(self, t):
            return list(self.pieces)

        def step(self, t, pieces=None):
            for i in self.pieces if pieces is None else pieces:
                for present, origin, side, onward in self.sides(t):

                    @pl.when(present)
                    def _():
                        self.along(origin, i, 1).wait_recv()

                        @pl.when(onward)
                        def _():
                            self.along(origin, i, side).start()

                        self.across(origin, i).start()

        def far_slab(self, origin):
            slab = self.rows_of(origin * INNER + (1 - b), 0, self.rows)
            remote(slab, slab, self.sent.at[1], self.far.at[origin], {"rows": other}).wait_recv()

        def rest(self, t):
            if t == 0:
                self.far_slab(a)
                return
            for present, origin, _, _ in self.sides(t):

                @pl.when(present)
                def _():
                    self.far_slab(origin)

        def sent_all(self, side, rows):
            part = self.buf.at[0:rows]
            remote(part, part, self.sent.at[side + 1], self.far.at[0], {"rows": other}).wait_send()

        def finish(self):
            for v in range(outer):

                @pl.when(a == v)
                def _():
                    self.sent_all(0, outer * self.rows)
                    if v + 1 < outer:
                        self.sent_all(1, (v + 1) * self.rows)
                    if v > 0:
                        self.sent_all(-1, (outer - v) * self.rows)

    def each_of(t, column, fn):
        if t == 0:
            fn(a * INNER + column)
            return
        for present, origin in ((a >= t, a - t), (a + t < outer, a + t)):

            @pl.when(present)
            def _():
                fn(origin * INNER + column)

    def each_near(t, fn):
        each_of(t, b, fn)

    def each_far(t, fn):
        each_of(t, 1 - b, fn)

    def each_slot(t, fn):
        if t == 0:
            fn(me)
            fn(other)
            return
        for present, origin in ((a >= t, a - t), (a + t < outer, a + t)):

            @pl.when(present)
            def _():
                fn(origin * INNER + b)
                fn(origin * INNER + (1 - b))

    near_half = outer // 2
    first = Gather(x_ref, lat, tokens, cut_rows(tokens, CUT1), sent1, near1, far1)
    second = Gather(chunk, rt, csp, cut_rows(csp, CUT2), sent2, near2, far2)

    def stat_copy(k):
        return remote(
            stat_own, stats.at[me], ss.at[0], ss.at[1], {"rows": lax.rem(me + k, ranks)}
        )

    def stat_all():
        part = stats.at[0 : ranks - 1]
        return remote(part, part, ss.at[0], ss.at[1], {"rows": other})

    def w_copy(k):
        dest = lax.rem(me + k, ranks)
        return remote(wt.at[dest], wbuf.at[me], ws.at[0], wr.at[me], {"rows": dest})

    def w_slot(k):
        return lax.rem(me + ranks - k, ranks)

    def w_pass_on(k, j, where):
        slot = w_slot(k)
        return remote(wbuf.at[slot], wbuf.at[slot], ws.at[j], wr.at[slot], where)

    def w_arrived(k):
        w_pass_on(k, 1, {"rows": other}).wait_recv()

    def w_to_core(k):
        return w_pass_on(k, 1, {"particle": grp * CORES + (1 - core)})

    def w_to_group(k, g):
        return w_pass_on(k, 1 + g, {"particle": lax.rem(grp + g, groups) * CORES + core})

    with jax.named_scope("start"):
        loads[3].wait()
        first.begin(first.pieces[:1])
        x32 = x_ref[...].astype(f32)
        sums = jnp.concatenate(
            [
                jnp.sum(x32, axis=0, keepdims=True),
                jnp.sum(x32 * x32, axis=0, keepdims=True),
                jnp.zeros((6, chans), f32),
            ],
            axis=0,
        )
        stat_own[...] = jnp.dot(sums, to_group, precision=HIGH, preferred_element_type=f32)
        stats[me] = stat_own[...]
        for k in range(1, ranks):
            stat_copy(k).start()
        first.begin(first.pieces[1:])

    with jax.named_scope("turn"):
        loads[0].wait()
        turned = wz[...].T
        for d in range(ranks):
            wt[d, 0:cs] = turned[d * cs : (d + 1) * cs]
            if csp != cs:
                wt[d, cs:csp] = jnp.zeros((csp - cs, wt.shape[2]), bf16)

    with jax.named_scope("start2"):
        for k in range(1, particles):

            @pl.when(mine == k % particles)
            def _():
                w_copy(k).start()

        for k in range(particles, ranks):

            @pl.when(mine == k % particles)
            def _():
                w_copy(k).start()

        first.keep()
        wbuf[me] = wt[me]

    def w_forward(k):
        q = k % particles

        @pl.when(mine == q)
        def _():
            w_arrived(k)
            for g in range(1, groups):
                w_to_group(k, g).start()
            w_to_core(k).start()

    def w_relay(k):
        q = k % particles

        @pl.when((core == q % CORES) & (grp != q // CORES))
        def _():
            w_arrived(k)
            w_to_core(k).start()

    def w_last(k):
        q = k % particles

        @pl.when(core != q % CORES)
        def _():
            w_arrived(k)

    low_end = a < near_half
    with jax.named_scope("kvw"):
        loads[1].wait()
        if cpad != chans:
            wqkv[...] = jnp.zeros_like(wqkv)
            for d in range(ranks):
                wqkv[d * csp : d * csp + cs] = wpad[d * cs : (d + 1) * cs]
        late = INNER * csp
        near_size = cpad // 2
        parts = (
            (jnp.where(low_end, 0, near_size), near_size, wnear),
            (jnp.where(low_end, near_size, late), near_size - late, wmid),
            (jnp.where(low_end, cpad - late, 0), late, wlate),
        )
        parts = [(pl.multiple_of(at, GRAIN), size, dst) for at, size, dst in parts]
        for at, size, dst in parts:
            for n in range(2 * tiles):
                dst[n * LANES : (n + 1) * LANES] = wqkv[
                    pl.ds(at, size), chans + n * LANES : chans + (n + 1) * LANES
                ].T
    with jax.named_scope("g1a"):
        for t in range(1, near_half):
            first.step(t)
    with jax.named_scope("stats"):
        stat_all().wait_recv()
        by_group = jnp.sum(stats[...], axis=0) / count
        mean_g = by_group[0:1]
        inverse = lax.rsqrt(by_group[1:2] - mean_g * mean_g + 1e-05)
        back = jnp.concatenate([mean_g, inverse, jnp.zeros((6, LANES), f32)], axis=0)
        spread = jnp.dot(back, to_chan, precision=HIGH, preferred_element_type=f32)
        mean_c, inverse_c = spread[0:1], spread[1:2]
        loads[4].wait()
        loads[5].wait()
        gain = 1.0 + scale_ref[...].reshape(1, chans)
        bias = shift_ref[...].reshape(1, chans)

    def activate(slot):
        at = pl.ds(pl.multiple_of(slot * tokens, GRAIN), tokens)
        v = lat[at].astype(f32)
        v = (v - mean_c) * inverse_c * gain + bias
        act[at] = (v / (1.0 + jnp.exp(-v))).astype(bf16)

    half = total // 2
    mine_half = lax.div(a, near_half)

    def conv(which):
        at = pl.multiple_of(which * half, LANES)
        yt[:, pl.ds(at, half)] = lax.dot_general(
            wd[...], act[pl.ds(at, half)], NT, preferred_element_type=f32
        )

    with jax.named_scope("own"):
        activate(me)
    with jax.named_scope("wf1"):
        for k in range(1, min(particles, ranks)):
            w_forward(k)
    with jax.named_scope("g1b0"):
        for t in range(near_half, outer - 1):
            first.step(t, first.order(t)[:1])
    with jax.named_scope("wf2"):
        for k in range(particles, ranks):
            w_forward(k)
    with jax.named_scope("g1b1"):
        for t in range(near_half, outer - 1):
            first.step(t, first.order(t)[1:])
    with jax.named_scope("act1"):
        first.rest(0)
        activate(other)
        for t in range(1, near_half):
            first.rest(t)
            each_slot(t, activate)
    with jax.named_scope("g1c"):
        first.step(outer - 1)
    with jax.named_scope("w2"):
        for k in range(1, ranks):
            w_relay(k)
    with jax.named_scope("act2"):
        for t in range(near_half, outer - 1):
            first.rest(t)
            each_slot(t, activate)
    with jax.named_scope("w3"):
        for k in range(1, ranks):
            w_last(k)
    with jax.named_scope("wd"):
        line = jnp.concatenate([wbuf[r][:, :share] for r in range(ranks)], axis=1)
        for tap in range(TAPS):
            wd[tap * csp : (tap + 1) * csp] = line[:, tap * chans : (tap + 1) * chans]
    with jax.named_scope("conv1"):
        conv(mine_half)
    with jax.named_scope("act3"):
        first.rest(outer - 1)
        each_slot(outer - 1, activate)
    with jax.named_scope("conv2"):
        pick = lax.broadcasted_iota(jnp.int32, (csp, chans), 0)
        at = lax.broadcasted_iota(jnp.int32, (csp, chans), 1)
        pick = jnp.where((at == me * cs + pick) & (pick < cs), 1.0, 0.0).astype(bf16)
        field[...] = lax.dot_general(pick, lat[...], NT, preferred_element_type=f32)
        conv(1 - mine_half)

    with jax.named_scope("taps"):
        lane = lax.broadcasted_iota(jnp.int32, (1, total), 1)
        column = lax.rem(lane, width)
        has_left = column > 0
        has_right = column < width - 1
        has_above = lane >= width
        has_below = lane < total - width

        def add_taps(i, carry):
            def tap(row, col):
                base = (row * 3 + col) * csp
                return yt[pl.ds(pl.multiple_of(base + i * GRAIN, GRAIN), GRAIN), :]

            cols = []
            for col in range(3):
                above = jnp.where(has_above, pltpu.roll(tap(0, col), width, 1), 0.0)
                below = jnp.where(has_below, pltpu.roll(tap(2, col), total - width, 1), 0.0)
                cols.append(tap(1, col) + above + below)
            left = jnp.where(has_left, pltpu.roll(cols[0], 1, 1), 0.0)
            right = jnp.where(has_right, pltpu.roll(cols[2], total - 1, 1), 0.0)
            at = pl.ds(pl.multiple_of(i * GRAIN, GRAIN), GRAIN)
            chunk[at] = (field[at] + (cols[1] + left + right)).astype(bf16)
            return carry

        for i in second.pieces:
            start, size = second.cuts[i]
            lax.fori_loop(start // GRAIN, (start + size) // GRAIN, add_taps, 0)
            second.begin([i])
        second.keep()

    own_r = lax.broadcasted_iota(jnp.int32, (csp, csp), 0)
    own_c = lax.broadcasted_iota(jnp.int32, (csp, csp), 1)
    same = (lax.div(own_r, per_group) == lax.div(own_c, per_group)) & (own_r < cs) & (own_c < cs)
    same = jnp.where(same, 1.0, 0.0).astype(f32)
    lane = lax.broadcasted_iota(jnp.int32, (csp, LANES), 1)

    def norm_copy(k):
        return remote(
            norm_own, norms.at[me], ns.at[0], nr.at[me], {"rows": lax.rem(me + k, ranks)}
        )

    with jax.named_scope("own"):
        v = chunk[...].astype(f32)
        both = jnp.where(
            lane == 0,
            jnp.sum(v, axis=1, keepdims=True),
            jnp.where(lane == 1, jnp.sum(v * v, axis=1, keepdims=True), 0.0),
        )
        both = jnp.dot(same, both, precision=HIGH, preferred_element_type=f32) / count
        mean = both[:, 0:1]
        inv = lax.rsqrt(both[:, 1:2] - mean * mean + 1e-05)
        both = jnp.where(lane == 0, mean, jnp.where(lane == 1, inv, 0.0))
        both = jnp.concatenate([both, jnp.zeros((LANES - csp, LANES), f32)], axis=0)
        norm_own[...] = both.T[0:8]
        for k in range(1, ranks):
            norm_copy(k).start()
        nt[pl.ds(pl.multiple_of(me * csp, GRAIN), csp)] = ((v - mean) * inv).astype(bf16)

    def normalize(slot):
        at = pl.ds(pl.multiple_of(slot * csp, GRAIN), csp)
        remote(norm_own, norms.at[slot], ns.at[0], nr.at[slot], {"rows": other}).wait_recv()
        both = norms[slot].T
        v = rt[at].astype(f32)
        nt[at] = ((v - both[:csp, 0:1]) * both[:csp, 1:2]).astype(bf16)

    step = 2 * LANES
    kv_rows = [slice(n * step, (n + 1) * step) for n in range(2 * chans // step)]

    def kv_part(i, rows):
        at, size, weights = parts[i]
        return jnp.dot(weights[rows], nt[pl.ds(at, size)], preferred_element_type=f32)

    with jax.named_scope("g2"):
        for t in range(1, outer):
            second.step(t)
            second.rest(t - 1)
            each_far(t - 1, normalize)
            each_near(t, normalize)
            if early and t == near_half:
                for rows in kv_rows:
                    kacc[rows] = kv_part(0, rows)

    with jax.named_scope("kv1"):
        row = lax.broadcasted_iota(jnp.int32, (tokens, total), 0)
        at = lax.broadcasted_iota(jnp.int32, (tokens, total), 1)
        pick = jnp.where(at == me * tokens + row, 1.0, 0.0).astype(bf16)

        def query_part(i):
            at, size, _ = parts[i]
            at = pl.ds(at, size)
            own = lax.dot_general(pick, nt[at], NT, preferred_element_type=f32).astype(bf16)
            return jnp.dot(own, wqkv[at, :chans], preferred_element_type=f32)

        query = query_part(0) + query_part(1)
        if cpad == chans:
            ahead = pl.ds(pl.multiple_of(jnp.where(low_end, 0, late), GRAIN), cpad - late)
            own = lax.dot_general(pick, rt[ahead], NT, preferred_element_type=f32)

            @pl.when(low_end)
            def _():
                own_rows[:, : chans - late] = own

            @pl.when(jnp.logical_not(low_end))
            def _():
                own_rows[:, late:] = own

        if early:
            for rows in kv_rows:
                kacc[rows] += kv_part(1, rows)
    with jax.named_scope("g2b"):
        second.rest(outer - 1)
        each_far(outer - 1, normalize)

    with jax.named_scope("qkv"):
        query = (query + query_part(2)).astype(bf16)
        if fold:
            query = (query.astype(f32) * head_dim ** (-0.5)).astype(bf16)
        for rows in kv_rows:
            head = kacc[rows] if early else kv_part(0, rows) + kv_part(1, rows)
            kvt[rows] = (head + kv_part(2, rows)).astype(bf16)
        if cpad == chans:
            own = lax.dot_general(
                pick, rt[pl.ds(parts[2][0], late)], NT, preferred_element_type=f32
            )

            @pl.when(low_end)
            def _():
                own_rows[:, chans - late :] = own

            @pl.when(jnp.logical_not(low_end))
            def _():
                own_rows[:, :late] = own

        else:
            resid = lax.dot_general(pick, rt[...], NT, preferred_element_type=f32)
            own_rows[...] = jnp.concatenate(
                [resid[:, d * csp : d * csp + cs] for d in range(ranks)], axis=1
            )

    with jax.named_scope("attn"):
        pair = 2 * head_dim
        lane = lax.broadcasted_iota(jnp.int32, (tokens, pair), 1)
        low = lane < head_dim
        zero = jnp.zeros((tokens, pair), bf16)
        for h in range(HEADS // 2):
            q = query[:, h * pair : (h + 1) * pair]
            q = jnp.concatenate([jnp.where(low, q, zero), jnp.where(low, zero, q)], axis=0)
            scores = jnp.dot(
                q, kvt[h * pair : (h + 1) * pair], preferred_element_type=f32
            )
            if not fold:
                scores = scores * (head_dim ** (-0.5))
            top = jnp.max(scores, axis=1, keepdims=True)
            weights = jnp.exp(scores - top)
            norm = jnp.sum(weights, axis=1, keepdims=True)
            mixed = (
                lax.dot_general(
                    weights.astype(bf16),
                    kvt[chans + h * pair : chans + (h + 1) * pair],
                    NT,
                    preferred_element_type=f32,
                )
                / norm
            )
            att[:, h * pair : (h + 1) * pair] = jnp.where(
                low, mixed[:tokens], mixed[tokens:]
            ).astype(bf16)
    def to_core(p, j):
        where = {"particle": grp * CORES + (1 - core)}
        return remote(blocks.at[p * tiles + j], blocks.at[p * tiles + j], ps.at[0], pr.at[0], where)

    def to_group(j, g, cross=0):
        there = 1 - core if cross else core
        where = {"particle": lax.rem(grp + g, groups) * CORES + there}
        recv = pr.at[1] if cross else pr.at[2 + (g - 1) * tiles + j]
        return remote(blocks.at[mine * tiles + j], blocks.at[mine * tiles + j], ps.at[groups if cross else g], recv, where)

    def from_group(j, g):
        part = blocks.at[of_group(g, core) * tiles + j]
        remote(part, part, ps.at[g], pr.at[2 + (g - 1) * tiles + j], {"rows": other}).wait_recv()

    def tiles_of(n, sem, recv=0):
        part = blocks.at[0:n]
        return remote(part, part, ps.at[sem], pr.at[recv], {"rows": other})

    passed = max(0, tiles - STRAIGHT)
    by_core = tiles + (groups - 1) * passed
    crossing = (groups - 1) * (tiles - passed)

    def of_group(g, side):
        return lax.rem(grp + groups - g, groups) * CORES + side

    with jax.named_scope("proj"):
        loads[2].wait()
        for j in range(tiles):
            if j % WIDE == 0:
                at = slice(j * LANES, min(j + WIDE, tiles) * LANES)
                wide = own_rows[:, at] + jnp.dot(
                    att[...], wout[:, at], preferred_element_type=f32
                )
            at = j % WIDE * LANES
            blocks[mine * tiles + j] = wide[:, at : at + LANES].astype(bf16)
            for g in range(1, groups):
                to_group(j, g).start()
            to_core(mine, j).start()
        for j in range(passed, tiles):
            for g in range(1, groups):
                to_group(j, g, 1).start()

    with jax.named_scope("resample"):
        for j in range(tiles):
            for g in range(1, groups):
                from_group(j, g)
                if j < passed:
                    to_core(of_group(g, core), j).start()
        tiles_of(by_core, 0).wait_recv()
        if crossing:
            tiles_of(crossing, 0, 1).wait_recv()
        for j in range(tiles):
            out_ref[:, j * LANES : (j + 1) * LANES] = blocks[anc_ref[mine] * tiles + j]
    with jax.named_scope("drain"):
        tiles_of(by_core, 0).wait_send()
        for g in range(1, groups):
            tiles_of(tiles, g).wait_send()
        if crossing:
            tiles_of(crossing, groups).wait_send()
        first.finish()
        second.finish()
        stat_all().wait_send()
        part = norms.at[0 : ranks - 1]
        remote(part, part, ns.at[0], nr.at[0], {"rows": other}).wait_send()
        for q in range(particles):
            count = len(range(q, ranks, particles)) - (q == 0)

            @pl.when(mine == q)
            def _():
                part = wbuf.at[0:count]
                for g in [0] + list(range(2, groups + 1)):
                    remote(part, part, ws.at[g], wr.at[0], {"rows": other}).wait_send()

        for c in range(CORES):
            count = sum(k % particles % CORES == c for k in range(1, ranks))

            @pl.when(core == c)
            def _():
                part = wbuf.at[0:count]
                remote(part, part, ws.at[1], wr.at[0], {"rows": other}).wait_send()


def per_device(latent, ada_scale, ada_shift, conv_weight, qkv_weight, out_weight, ancestors):
    _, rows_here, width, chans = latent.shape
    tokens = rows_here * width
    ranks = lax.axis_size("rows")
    particles = lax.axis_size("particle")
    groups = particles // CORES
    total = tokens * ranks
    share = conv_weight.shape[0]
    span = -(-share // LANES) * LANES
    if share % GRAIN:
        conv_weight = jnp.pad(conv_weight, ((0, span - share), (0, 0)))
    cs = chans // ranks
    csp = -(-cs // GRAIN) * GRAIN
    cpad = csp * ranks
    outer = ranks // INNER
    n1, n2 = len(cut_rows(tokens, CUT1)), len(cut_rows(csp, CUT2))
    early = outer <= 4
    dims = (rows_here, width, chans, ranks, particles, share, early)
    bf16, f32 = jnp.bfloat16, jnp.float32
    dma = pltpu.SemaphoreType.DMA
    out = pl.pallas_call(
        functools.partial(kernel, dims),
        out_shape=pltpu.VMEM((tokens, chans), bf16),
        in_specs=[pl.BlockSpec(memory_space=pltpu.SMEM)]
        + [pl.BlockSpec(memory_space=pl.ANY)] * 6,
        out_specs=pl.BlockSpec(memory_space=pltpu.VMEM),
        scratch_shapes=[
            pltpu.VMEM((tokens, chans), bf16),
            pltpu.VMEM(ada_scale.shape, f32),
            pltpu.VMEM(ada_shift.shape, f32),
            pltpu.VMEM((span, chans), bf16),
            pltpu.VMEM((ranks, csp, span), bf16),
            pltpu.VMEM((ranks, csp, span), bf16),
            pltpu.VMEM((TAPS * csp, chans), bf16),
            pltpu.VMEM((cpad, 3 * chans), bf16),
            pltpu.VMEM((GRAIN, LANES) if cpad == chans else qkv_weight.shape, bf16),
            pltpu.VMEM((2 * chans, cpad // 2), bf16),
            pltpu.VMEM((2 * chans, cpad // 2 - INNER * csp), bf16),
            pltpu.VMEM((2 * chans, INNER * csp), bf16),
            pltpu.VMEM((2 * chans, total) if early else (8, LANES), f32),
            pltpu.VMEM(out_weight.shape, bf16),
            pltpu.VMEM((total, chans), bf16),
            pltpu.VMEM((total, chans), bf16),
            pltpu.VMEM((TAPS * csp, total), f32),
            pltpu.VMEM((csp, total), f32),
            pltpu.VMEM((csp, total), bf16),
            pltpu.VMEM((cpad, total), bf16),
            pltpu.VMEM((cpad, total), bf16),
            pltpu.VMEM((2 * chans, total), bf16),
            pltpu.VMEM((tokens, chans), bf16),
            pltpu.VMEM((tokens, chans), f32),
            pltpu.VMEM((particles * (chans // LANES), tokens, LANES), bf16),
            pltpu.VMEM((8, LANES), f32),
            pltpu.VMEM((ranks, 8, LANES), f32),
            pltpu.VMEM((8, LANES), f32),
            pltpu.VMEM((ranks, 8, LANES), f32),
            dma((6,)),
            dma((1,)),
            dma((ranks,)),
            dma((1 + groups,)),
            dma((ranks,)),
            dma((2,)),
            dma((3,)),
            dma((outer, n1)),
            dma((outer,)),
            dma((3,)),
            dma((outer, n2)),
            dma((outer,)),
            dma((groups + 1,)),
            dma((2 + (groups - 1) * (chans // LANES),)),
        ],
        compiler_params=pltpu.CompilerParams(
            collective_id=0, has_side_effects=True, vmem_limit_bytes=64000 * 1024
        ),
        name="block",
    )(
        ancestors,
        latent.reshape(tokens, chans),
        ada_scale,
        ada_shift,
        conv_weight,
        qkv_weight,
        out_weight,
    )
    return out.reshape(latent.shape)


def solution(mesh):
    in_specs = (P("particle", "rows", None, None), P(), P(), P("rows", None), P(), P(), P())
    out_specs = P("particle", "rows", None, None)
    return jax.shard_map(
        per_device, mesh=mesh, in_specs=in_specs, out_specs=out_specs, check_vma=False
    )
```
